256 devices in a mesh: section: 32 (over x, z), expert: 8 (over y, core).
Axes of the slice: x: 4, y: 4, z: 8, core: 2. Of those that a mesh axis runs over, the one named last changes fastest.
Arguments:
- tokens: bfloat16 [2048, 4096], P('expert', 'section'), may hold values from -6 to 6
- routes: int32 [2048, 2], P('expert'), may hold values from 0 to 7, all different within a row; in each aligned block of 256 rows (0 to 255, 256 to 511, ...) at most 80 rows name the same one
- mix_weights: float32 [2048, 2], P('expert'), may hold values from 0.2 to 1
- w_gate: bfloat16 [8, 4096, 8192], P('expert', None, 'section'), may hold values from -0.1875 to 0.1875
- w_up: bfloat16 [8, 4096, 8192], P('expert', None, 'section'), may hold values from -0.1875 to 0.1875
- w_down: bfloat16 [8, 8192, 4096], P('expert', 'section'), may hold values from -0.125 to 0.125
- upstream: bfloat16 [2048, 4096], P('expert', 'section'), may hold values from -6 to 6
Outputs:
- mixed: bfloat16 [2048, 4096], P('expert', 'section')
- grad_tokens: bfloat16 [2048, 4096], P('expert', 'section')
- grad_mix: float32 [2048, 2], P('expert')
- grad_gate: bfloat16 [8, 4096, 8192], P('expert', None, 'section')
- grad_up: bfloat16 [8, 4096, 8192], P('expert', None, 'section')
- grad_down: bfloat16 [8, 8192, 4096], P('expert', 'section')
The draws below stay inside these ranges and needn't reach their ends.
Inputs may be any that keep to these rules, and one draw needn't show every extreme that they name: `routes`: each token names 2 different experts. Among the 256 tokens of one index of the expert axis no expert is named more than 80 times, and in some such block one expert is named exactly 80 times.
All inputs are finite; a program needn't handle non-finite values.
Results may differ from the reference program's by a relative error of at most 0.02.
Values may be sent and summed in bfloat16 or wider, within the bound.
No kernel may reach another device: no remote copies, remote signals or barrier semaphores. Data moves between devices by JAX's collectives and lax.ppermute only.
A program may use at most 128 MiB of HBM per device.

```python
import math
import jax
import jax.numpy as jnp
import numpy as np
from jax import lax

D = 4096
FF = 8192
NEXP = 8
TOP = 2
TOK_DEV = 256
CAP = 80
TOKENS = 2048
N_SECTION = 32
N_EXPERT = 8


def strengthened(entries, stream_key, source, target, blocks, factor):
    def block_of(dim):
        return (jnp.arange(entries.shape[dim]) // (entries.shape[dim] // blocks)).reshape((-1,) + (1,) * (entries.ndim - 1 - dim))

    near = jax.random.permutation(stream_key, blocks)[block_of(target)]
    far = (block_of(target) + blocks // 2) % blocks
    return jnp.where((block_of(source) == near) | (block_of(source) == far), factor * entries, entries)


def block_scale(key, dims, cuts, smallest, top_value):
    level, own = 1.0, jax.random.fold_in(key, 6)
    for dim, blocks in cuts:
        draws = jnp.exp(jax.random.uniform(jax.random.fold_in(own, dim), (blocks,), jnp.float32, smallest / len(cuts), top_value / len(cuts)))
        level = level * jnp.repeat(draws, dims[dim] // blocks).reshape([-1 if axis == dim else 1 for axis in range(len(dims))])
    return level


def routed_block(key, own, number, rows, number_of, top, bound, slope):
    sequence = jax.random.permutation(key, number_of)
    crowded, ordinary = portions_of(number_of, rows * top, bound, slope, True), portions_of(number_of, rows * top, bound, slope, False)
    places = jnp.arange(number_of)

    def named(tallies, rotation):
        used = int((tallies > 0).sum())
        fixed = max(1, used // 4)
        moved = fixed + (places - fixed + rotation * (used - fixed)) % max(1, number_of - fixed)
        return jnp.zeros((number_of,), jnp.int32).at[sequence[jnp.where(places < fixed, places, moved)]].set(jnp.asarray(tallies, jnp.int32))

    tallies = jnp.where(number % 4 == 0, named(crowded, number // 4), named(ordinary, number - number // 4 - 1))
    mixed = jax.random.permutation(jax.random.fold_in(own, 3), number_of)
    donor, receiver = mixed[0:number_of // 2 * 2:2], mixed[1:number_of // 2 * 2:2]
    slack = jnp.minimum(tallies[donor] - 1, bound - tallies[receiver]) // 2
    slack = jnp.where((donor == sequence[0]) | (receiver == sequence[0]) | (tallies[receiver] == 0), 0, jnp.maximum(slack, 0))
    moved = jax.random.randint(jax.random.fold_in(own, 4), (number_of // 2,), 0, 1 << 20) % (slack + 1)
    tallies = tallies.at[donor].add(-moved).at[receiver].add(moved)
    items = jnp.searchsorted(jnp.cumsum(tallies), jnp.arange(rows * top), side="right").astype(jnp.int32)
    listing = items.reshape(top, rows).T
    listing = listing[jax.random.permutation(jax.random.fold_in(own, 1), rows)]
    rotation = jax.random.randint(jax.random.fold_in(own, 2), (rows, 1), 0, top)
    return jnp.take_along_axis(listing, (jnp.arange(top)[None, :] + rotation) % top, axis=1)


def portions_of(amount, total, bound, lean, full):
    loads = [(1 << 20) // math.isqrt(grade ** lean) + 1 for grade in range(1, amount + 1)]
    largest = bound if full else min(bound, max(-(-total // amount), total * loads[0] // sum(loads)))
    least = 1 if total - largest >= amount - 1 else 0
    given, spare = [largest] + [least] * (amount - 1), total - largest - least * (amount - 1)
    while spare > 0:
        free = [i for i in range(1, amount) if given[i] < largest] or [i for i in range(1, amount) if given[i] < bound]
        whole, left = sum([loads[i] for i in free]), spare
        for i in free:
            extra = min(bound - given[i], max(1, left * loads[i] // whole), spare)
            given[i] = given[i] + extra
            spare = spare - extra
    return np.array(given)


def gaussian(own_key, dims, width, bound, cuts=(), held_as=jnp.bfloat16):
    result = jax.random.normal(own_key, dims, jnp.float32) * width
    if len(cuts) > 0:
        result = block_scale(own_key, dims, cuts, -0.22, 0.18) * result
    return jnp.clip(result, min=-bound, max=bound).astype(held_as)


def heavy_noise(own_key, extent, deviation, reach, pieces, heavy, kind=jnp.bfloat16):
    array = deviation * jax.random.normal(own_key, extent, jnp.float32)
    if pieces:
        array = array * block_scale(own_key, extent, pieces, -0.22, 0.18)
    return jnp.clip(strengthened(array, jax.random.fold_in(own_key, 3), *heavy), -reach, reach).astype(kind)


def setup_inputs(seed: int = 0) -> dict:
    key_list = jax.random.split(jax.random.key(seed), 8)
    tokens = gaussian(key_list[0], (TOKENS, D), 1.0, 6.0, ((0, 8), (1, 32)))
    routes_keys = jax.random.split(jax.random.fold_in(key_list[1], 1), TOKENS // TOK_DEV)
    routes_turns = jax.random.permutation(jax.random.fold_in(key_list[1], 3), TOKENS // TOK_DEV)
    routes = jax.vmap(lambda own, number: routed_block(jax.random.fold_in(key_list[1], 2), own, number, TOK_DEV, NEXP, TOP, CAP, 1))(routes_keys, routes_turns).reshape((TOKENS, TOP))
    mix_weights = jnp.clip(0.2 + 0.8 * jax.random.uniform(key_list[2], (TOKENS, TOP), jnp.float32) ** block_scale(key_list[2], (TOKENS, TOP), ((0, 8),), -0.2, 0.2), 0.2, 1.0)
    w_gate = heavy_noise(key_list[3], (NEXP, D, FF), D ** -0.5, 0.1875, ((0, 8), (2, 32)), (2, 1, 32, 2.75))
    w_up = heavy_noise(key_list[4], (NEXP, D, FF), D ** -0.5, 0.1875, ((0, 8), (2, 32)), (2, 1, 32, 2.75))
    w_down = heavy_noise(key_list[5], (NEXP, FF, D), FF ** -0.5, 0.125, ((0, 8), (1, 32)), (1, 2, 32, 2.75))
    upstream = gaussian(key_list[6], (TOKENS, D), 1.0, 6.0, ((0, 8), (1, 32)))
    return {"tokens": tokens, "routes": routes, "mix_weights": mix_weights, "w_gate": w_gate, "w_up": w_up, "w_down": w_down, "upstream": upstream}


highest = lax.Precision.HIGHEST


def slot_tables(route_rows, mix_rows, capacity, experts):
    tok_count, top_count = route_rows.shape
    flat_routes = route_rows.reshape(-1)
    onehot = (flat_routes[:, None] == jnp.arange(experts, dtype=jnp.int32)[None, :]).astype(jnp.int32)
    earlier = jnp.cumsum(onehot, axis=0) - onehot
    position = jnp.sum(earlier * onehot, axis=1)
    target = (flat_routes * capacity + position).reshape(tok_count, top_count)
    slot_ids = jnp.arange(experts * capacity, dtype=jnp.int32)
    matches = (target[None, :, :] == slot_ids[:, None, None]).astype(jnp.float32)
    select = jnp.sum(matches, axis=2)
    weighted = jnp.sum(matches * mix_rows[None, :, :], axis=2)
    return target, select, weighted


def group_sum(make_part, shape):
    def step(index, total):
        part = make_part(index).astype(jnp.bfloat16)
        part = lax.optimization_barrier(part)
        return total + part.astype(jnp.float32)
    return lax.fori_loop(0, N_SECTION, step, jnp.zeros(shape, jnp.float32))


def expert_pass(xin, grad_rows, gate_w, up_w, down_w):
    group_width = FF // N_SECTION
    row_count = xin.shape[0]
    act_gate = jnp.dot(xin, gate_w, preferred_element_type=jnp.float32)
    act_up = jnp.dot(xin, up_w, preferred_element_type=jnp.float32)
    sig = jax.nn.sigmoid(act_gate)
    silu_gate = act_gate * sig
    hidden = (silu_gate * act_up).astype(jnp.bfloat16)

    def out_part(index):
        start = index * group_width
        return jnp.dot(lax.dynamic_slice_in_dim(hidden, start, group_width, 1),
                       lax.dynamic_slice_in_dim(down_w, start, group_width, 0),
                       preferred_element_type=jnp.float32)

    expert_out = group_sum(out_part, (row_count, D)).astype(jnp.bfloat16)
    grad_hidden = lax.dot_general(grad_rows, down_w, (((1,), (1,)), ((), ())), preferred_element_type=jnp.float32)
    grad_down = lax.dot_general(hidden, grad_rows, (((0,), (0,)), ((), ())), preferred_element_type=jnp.float32).astype(jnp.bfloat16)
    dsilu = sig * (1.0 + act_gate * (1.0 - sig))
    grad_act_gate = (grad_hidden * act_up * dsilu).astype(jnp.bfloat16)
    grad_act_up = (grad_hidden * silu_gate).astype(jnp.bfloat16)
    grad_gate = lax.dot_general(xin, grad_act_gate, (((0,), (0,)), ((), ())), preferred_element_type=jnp.float32).astype(jnp.bfloat16)
    grad_up = lax.dot_general(xin, grad_act_up, (((0,), (0,)), ((), ())), preferred_element_type=jnp.float32).astype(jnp.bfloat16)

    def back_part(index):
        start = index * group_width
        first = lax.dot_general(lax.dynamic_slice_in_dim(grad_act_gate, start, group_width, 1),
                                lax.dynamic_slice_in_dim(gate_w, start, group_width, 1),
                                (((1,), (1,)), ((), ())), preferred_element_type=jnp.float32)
        second = lax.dot_general(lax.dynamic_slice_in_dim(grad_act_up, start, group_width, 1),
                                 lax.dynamic_slice_in_dim(up_w, start, group_width, 1),
                                 (((1,), (1,)), ((), ())), preferred_element_type=jnp.float32)
        return first + second

    grad_rows_in = group_sum(back_part, (row_count, D)).astype(jnp.bfloat16)
    return expert_out, grad_rows_in, grad_gate, grad_up, grad_down


def reference(tokens, routes, mix_weights, w_gate, w_up, w_down, upstream):
    blocks = N_EXPERT
    token_blocks = tokens.reshape(blocks, TOK_DEV, D)
    upstream_blocks = upstream.reshape(blocks, TOK_DEV, D)
    target, select, weighted = jax.vmap(lambda route_rows, mix_rows: slot_tables(route_rows, mix_rows, CAP, NEXP))(
        routes.reshape(blocks, TOK_DEV, TOP), mix_weights.reshape(blocks, TOK_DEV, TOP))
    sent = jnp.einsum("bst,btd->bsd", select, token_blocks.astype(jnp.float32), precision=highest).astype(jnp.bfloat16)
    grad_sent = jnp.einsum("bst,btd->bsd", weighted, upstream_blocks.astype(jnp.float32), precision=highest).astype(jnp.bfloat16)

    def to_experts(block):
        return block.reshape(blocks, NEXP, CAP, D).transpose(1, 0, 2, 3).reshape(NEXP, blocks * CAP, D)

    def to_sources(rows):
        return rows.reshape(NEXP, blocks, CAP, D).transpose(1, 0, 2, 3).reshape(blocks, NEXP * CAP, D)

    expert_out, grad_rows_in, grad_gate, grad_up, grad_down = lax.map(
        lambda items: expert_pass(*items), (to_experts(sent), to_experts(grad_sent), w_gate, w_up, w_down))
    returned = to_sources(expert_out).astype(jnp.float32)
    moe_out = jnp.einsum("bst,bsd->btd", weighted, returned, precision=highest)
    mixed = (token_blocks.astype(jnp.float32) + moe_out).astype(jnp.bfloat16).reshape(-1, D)
    picked = jax.vmap(lambda rows, index: rows[index])(returned, target)
    grad_mix = jnp.einsum("btkd,btd->btk", picked, upstream_blocks.astype(jnp.float32), precision=highest).reshape(-1, TOP)
    back_rows = to_sources(grad_rows_in).astype(jnp.float32)
    grad_moe = jnp.einsum("bst,bsd->btd", select, back_rows, precision=highest)
    grad_tokens = (upstream_blocks.astype(jnp.float32) + grad_moe).astype(jnp.bfloat16).reshape(-1, D)
    return (mixed, grad_tokens, grad_mix, grad_gate, grad_up, grad_down)
```

```python
import jax
import jax.numpy as jnp
from jax import lax
from jax.sharding import PartitionSpec as P

highest = lax.Precision.HIGHEST
NX, NZ = 4, 8


def z_shift(d):
    return [(x * NZ + z, x * NZ + (z + d) % NZ) for x in range(NX) for z in range(NZ)]


def x_shift(d):
    return [(x * NZ + z, ((x + d) % NX) * NZ + z) for x in range(NX) for z in range(NZ)]


Z_GROUPS = [[x * NZ + z for z in range(NZ)] for x in range(NX)]
X_GROUPS = [[x * NZ + z for x in range(NX)] for z in range(NZ)]


def shift_z(value, d):
    return lax.ppermute(value, "section", z_shift(d))


def shift_x(value, d):
    return lax.ppermute(value, "section", x_shift(d))


def in_order(relative, own, count):
    held = jnp.stack(relative)
    return [
        lax.dynamic_index_in_dim(held, (own - j) % count, 0, keepdims=False) for j in range(count)
    ]


def slot_tables(route_rows, mix_rows, capacity, experts):
    tok_count, top_count = route_rows.shape
    flat_routes = route_rows.reshape(-1)
    onehot = (flat_routes[:, None] == jnp.arange(experts, dtype=jnp.int32)[None, :]).astype(
        jnp.int32
    )
    earlier = jnp.cumsum(onehot, axis=0) - onehot
    position = jnp.sum(earlier * onehot, axis=1)
    target = (flat_routes * capacity + position).reshape(tok_count, top_count)
    slot_ids = jnp.arange(experts * capacity, dtype=jnp.int32)
    hits = target[None, :, :] == slot_ids[:, None, None]
    matches = hits.astype(jnp.float32)
    select = jnp.sum(matches, axis=2)
    weighted = jnp.sum(matches * mix_rows[None, :, :], axis=2)
    token_ids = jnp.arange(tok_count, dtype=jnp.int32)
    slot_token = jnp.sum(jnp.sum(hits.astype(jnp.int32), axis=2) * token_ids[None, :], axis=1)
    return (target, select, weighted, slot_token)


def per_device(tokens, routes, mix_weights, w_gate, w_up, w_down, upstream):
    experts = lax.axis_size("expert")
    section = lax.axis_index("section")
    my_x, my_z = section // NZ, section % NZ
    tok_count, feat = tokens.shape
    top_count = routes.shape[1]
    capacity = 5 * tok_count * top_count // (4 * experts)
    rows = experts * capacity
    f32, bf16 = jnp.float32, jnp.bfloat16
    target, select, weighted, slot_token = slot_tables(routes, mix_weights, capacity, experts)
    slot_fill = jnp.sum(select, axis=1)
    slot_scale = jnp.sum(weighted, axis=1)
    ff = w_gate.shape[2]
    both = jnp.concatenate([w_gate[0], w_up[0]], axis=1)
    both = both.reshape(NX, NZ, feat, 2 * ff).transpose(1, 0, 2, 3)
    both_z = both.reshape(NZ, NX * feat, 2 * ff)
    down_x = [w_down[0][:, j * NZ * feat : (j + 1) * NZ * feat] for j in range(NX)]

    def collect(source, factor):
        taken = source[slot_token].astype(f32)
        return (taken * factor[:, None]).astype(bf16)

    sent = jnp.concatenate([collect(tokens, slot_fill), collect(upstream, slot_scale)], axis=1)
    arrived = lax.all_to_all(
        sent.reshape(experts, capacity, 2 * feat), "expert", split_axis=0, concat_axis=0, tiled=True
    ).reshape(rows, 2 * feat)
    tok_rows, up_rows = arrived[:, :feat], arrived[:, feat:]

    pieces = in_order([tok_rows] + [shift_x(tok_rows, d) for d in (1, 2, 3)], my_x, NX)
    tok_x = jnp.concatenate(pieces, axis=1)
    dispatched = lax.all_gather(
        tok_x, "section", axis_index_groups=Z_GROUPS, axis=1, tiled=True
    )

    pieces = in_order([up_rows] + [shift_z(up_rows, d) for d in range(1, NZ)], my_z, NZ)
    up_z = jnp.concatenate(pieces, axis=1)
    grad_rows = in_order([up_z] + [shift_x(up_z, d) for d in (1, 2, 3)], my_x, NX)

    act = jnp.dot(dispatched, both_z.reshape(-1, 2 * ff), preferred_element_type=f32)
    act_gate, act_up = act[:, :ff], act[:, ff:]
    sig = jax.nn.sigmoid(act_gate)
    silu_gate = act_gate * sig
    hidden = (silu_gate * act_up).astype(bf16)
    partial_out = jnp.concatenate(
        [jnp.dot(hidden, part, preferred_element_type=f32).astype(bf16) for part in down_x], axis=0
    )
    summed = lax.psum_scatter(
        partial_out, "section", axis_index_groups=X_GROUPS, scatter_dimension=0, tiled=True
    )
    summed = summed.reshape(rows, NZ, feat).transpose(1, 0, 2).reshape(NZ * rows, feat)
    summed = lax.psum_scatter(
        summed, "section", axis_index_groups=Z_GROUPS, scatter_dimension=0, tiled=True
    )

    def to_sources(value):
        back = lax.all_to_all(
            value.reshape(experts, capacity, feat), "expert", split_axis=0, concat_axis=0, tiled=True
        )
        return back.reshape(rows, feat)

    returned = to_sources(summed).astype(f32)
    moe_out = jnp.dot(weighted.T, returned, precision=highest)
    mixed = (tokens.astype(f32) + moe_out).astype(bf16)
    picked = returned[target]
    upstream_wide = upstream.astype(f32)
    grad_mix = jnp.einsum("tkd,td->tk", picked, upstream_wide, precision=highest)
    for d in (2, 1):
        grad_mix = grad_mix + shift_x(grad_mix, d)
    for d in (4, 2, 1):
        grad_mix = grad_mix + shift_z(grad_mix, d)

    grad_hidden = sum(
        lax.dot_general(part, weight, (((1,), (1,)), ((), ())), preferred_element_type=f32)
        for part, weight in zip(grad_rows, down_x)
    )
    dsilu = sig * (1.0 + act_gate * (1.0 - sig))
    grad_act = jnp.concatenate(
        [(grad_hidden * act_up * dsilu).astype(bf16), (grad_hidden * silu_gate).astype(bf16)], axis=1
    )

    def back_part(d):
        weight = lax.dynamic_index_in_dim(both_z, (my_z + d) % NZ, 0, keepdims=False)
        return lax.dot_general(
            grad_act, weight, (((1,), (1,)), ((), ())), preferred_element_type=f32
        )

    half = rows // 2
    far = back_part(4).astype(bf16)
    right, left = shift_z(far[:half], 1), shift_z(far[half:], -1)
    for d in (3, 2, 1):
        ahead, behind = back_part(d), back_part(-d)
        if d == 3:
            ahead = jnp.concatenate([ahead[:half] + right.astype(f32), ahead[half:]])
            behind = jnp.concatenate([behind[:half], behind[half:] + left.astype(f32)])
        else:
            ahead, behind = ahead + right.astype(f32), behind + left.astype(f32)
        right, left = shift_z(ahead.astype(bf16), 1), shift_z(behind.astype(bf16), -1)
    total = back_part(0) + right.astype(f32) + left.astype(f32)
    by_x = total.reshape(rows, NX, feat).transpose(1, 0, 2)
    back_sum = lax.dynamic_index_in_dim(by_x, my_x, 0, keepdims=False)
    for d in (1, 2, 3):
        part = lax.dynamic_index_in_dim(by_x, (my_x + d) % NX, 0, keepdims=False).astype(bf16)
        back_sum = back_sum + shift_x(part, d).astype(f32)

    grad_down = jnp.concatenate(
        [
            lax.dot_general(hidden, part, (((0,), (0,)), ((), ())), preferred_element_type=f32)
            for part in grad_rows
        ],
        axis=1,
    ).astype(bf16)
    grad_both = lax.dot_general(
        dispatched, grad_act, (((0,), (0,)), ((), ())), preferred_element_type=f32
    ).astype(bf16)
    grad_both = grad_both.reshape(NZ, NX, feat, 2 * ff).transpose(1, 0, 2, 3).reshape(-1, 2 * ff)
    back_rows = to_sources(back_sum.astype(bf16)).astype(f32)
    grad_moe = jnp.dot(select.T, back_rows, precision=highest)
    grad_tokens = (upstream_wide + grad_moe).astype(bf16)
    return (
        mixed,
        grad_tokens,
        grad_mix,
        grad_both[None, :, :ff],
        grad_both[None, :, ff:],
        grad_down[None],
    )


def solution(mesh):
    return jax.shard_map(
        per_device,
        mesh=mesh,
        in_specs=(
            P("expert", "section"),
            P("expert", None),
            P("expert", None),
            P("expert", None, "section"),
            P("expert", None, "section"),
            P("expert", "section", None),
            P("expert", "section"),
        ),
        out_specs=(
            P("expert", "section"),
            P("expert", "section"),
            P("expert", None),
            P("expert", None, "section"),
            P("expert", None, "section"),
            P("expert", "section", None),
        ),
        check_vma=False,
    )
```

```python
import functools

import jax
import jax.numpy as jnp
from jax import lax
from jax.experimental import pallas as pl
from jax.experimental.pallas import tpu as pltpu
from jax.sharding import PartitionSpec as P

highest = lax.Precision.HIGHEST
f32, bf16 = jnp.float32, jnp.bfloat16
NX, NZ = 4, 8
Z_GROUPS = [[x * NZ + z for z in range(NZ)] for x in range(NX)]


def shift_z(value, d):
    pairs = [(x * NZ + z, x * NZ + (z + d) % NZ) for x in range(NX) for z in range(NZ)]
    return lax.ppermute(value, "section", pairs)


def shift_x(value, d):
    pairs = [(x * NZ + z, ((x + d) % NX) * NZ + z) for x in range(NX) for z in range(NZ)]
    return lax.ppermute(value, "section", pairs)


def in_order(relative, own, count):
    held = jnp.stack(relative)
    return jnp.concatenate(
        [lax.dynamic_index_in_dim(held, (own - j) % count, 0, keepdims=False) for j in range(count)],
        axis=1,
    )


def spread_x(value, own):
    parts = value.reshape(value.shape[0], NX, -1).transpose(1, 0, 2)

    def part(d):
        return lax.dynamic_index_in_dim(parts, (own + d) % NX, 0, keepdims=False)

    sent = [shift_x(part(d).astype(bf16), d) for d in range(1, NX)]
    return sum((term.astype(f32) for term in sent), part(0))


def spread_z(value, own):
    parts = value.reshape(value.shape[0], NZ, -1).transpose(1, 0, 2)

    def part(d):
        return lax.dynamic_index_in_dim(parts, (own + d) % NZ, 0, keepdims=False)

    above = shift_z(jnp.stack([part(2), part(3), part(4)]).astype(bf16), 3).astype(f32)
    below = shift_z(jnp.stack([part(-3), part(-2)]).astype(bf16), -3).astype(f32)
    right = shift_z((part(1) + above[2] + below[1]).astype(bf16), 1)
    left = shift_z((part(-1) + above[0]).astype(bf16), -1)
    return part(0) + above[1] + below[0] + right.astype(f32) + left.astype(f32)


def near_z(value):
    return jnp.stack([shift_z(value, 1), value, shift_z(value, -1)])


def far_z(near):
    low, high = shift_z(near, 3), shift_z(near[:2], -3)
    return [low, near, high]


def side_by_side(pieces, own):
    held = jnp.concatenate(pieces)
    return jnp.concatenate(
        [
            lax.dynamic_index_in_dim(held, (j - own + 4) % NZ, 0, keepdims=False)
            for j in range(NZ)
        ],
        axis=1,
    )


def dot_nt(a, b):
    return lax.dot_general(a, b, (((1,), (1,)), ((), ())), preferred_element_type=f32)


def dot_tn(a, b):
    return lax.dot_general(a, b, (((0,), (0,)), ((), ())), preferred_element_type=f32)


def forward_kernel(
    x_ref, tok_ref, gate_ref, up_ref, down_ref, coef_ref, silu_ref, hid_ref, *rest
):
    outs, (acc_gate, acc_up) = rest[:NX], rest[NX:]
    step = pl.program_id(0)
    width = gate_ref.shape[-1]

    @pl.when(step == 0)
    def _():
        acc_gate[...] = jnp.zeros_like(acc_gate)
        acc_up[...] = jnp.zeros_like(acc_up)

    @pl.when(step < NZ)
    def _():
        block = tok_ref[...]
        gate = gate_ref[...].reshape(-1, width)
        up = up_ref[...].reshape(-1, width)
        acc_gate[...] += jnp.dot(block, gate, preferred_element_type=f32)
        acc_up[...] += jnp.dot(block, up, preferred_element_type=f32)

    @pl.when(step == NZ - 1)
    def _():
        act_gate, act_up = acc_gate[...], acc_up[...]
        sig = jax.nn.sigmoid(act_gate)
        silu_gate = act_gate * sig
        silu_ref[...] = silu_gate
        coef_ref[...] = act_up * (sig * (1.0 + act_gate * (1.0 - sig)))
        hid_ref[...] = (silu_gate * act_up).astype(bf16)

    for d in range(NX):

        @pl.when(step == NZ + d)
        def _(d=d):
            outs[d][...] = jnp.dot(
                hid_ref[...], down_ref[...], preferred_element_type=f32
            ).astype(bf16)


def backward_kernel(x_ref, *refs):
    ups = refs[:NX]
    down_ref, gate_ref, up_ref, coef_ref, silu_ref, hid_ref = refs[NX : NX + 6]
    part_ref, gate_out, up_out, mix_out, acc = refs[NX + 6 :]
    step = pl.program_id(0)
    width = gate_ref.shape[-1]

    for d in range(NX):

        @pl.when(step == d)
        def _(d=d):
            term = dot_nt(ups[d][...], down_ref[...])
            acc[...] = term if d == 0 else acc[...] + term

    @pl.when(step == NX - 1)
    def _():
        grad_hidden = acc[...]
        gate_out[...] = (grad_hidden * coef_ref[...]).astype(bf16)
        up_out[...] = (grad_hidden * silu_ref[...]).astype(bf16)
        terms = jnp.sum(grad_hidden * hid_ref[...].astype(f32), axis=1, keepdims=True)
        mix_out[...] = jnp.broadcast_to(terms, mix_out.shape)

    @pl.when(step >= NX)
    def _():
        gate = gate_ref[...].reshape(-1, width)
        up = up_ref[...].reshape(-1, width)
        part_ref[0] = (dot_nt(gate_out[...], gate) + dot_nt(up_out[...], up)).astype(bf16)


def weight_kernel(x_ref, *refs):
    tok_ref, gact_ref, uact_ref, hid_ref = refs[:4]
    ups = refs[4 : 4 + NX]
    gate_out, up_out, down_out = refs[4 + NX :]
    step = pl.program_id(0)

    @pl.when(step < NZ)
    def _():
        block = tok_ref[...]
        gate_out[...] = dot_tn(block, gact_ref[...]).astype(bf16).reshape(gate_out.shape)
        up_out[...] = dot_tn(block, uact_ref[...]).astype(bf16).reshape(up_out.shape)

    for d in range(NX):

        @pl.when(step == NZ + d)
        def _(d=d):
            down_out[...] = dot_tn(hid_ref[...], ups[d][...]).astype(bf16)


def call(kernel, steps, in_specs, out_specs, out_shape, scratch, flops, moved, args):
    return pl.pallas_call(
        kernel,
        grid_spec=pltpu.PrefetchScalarGridSpec(
            num_scalar_prefetch=1,
            grid=(steps,),
            in_specs=in_specs,
            out_specs=out_specs,
            scratch_shapes=scratch,
        ),
        out_shape=out_shape,
        compiler_params=pltpu.CompilerParams(vmem_limit_bytes=50 * 1024 * 1024),
        cost_estimate=pl.CostEstimate(flops=flops, bytes_accessed=moved, transcendentals=0),
    )(*args)


def slot_tables(route_rows, mix_rows, capacity, experts):
    tok_count, top_count = route_rows.shape
    flat_routes = route_rows.reshape(-1)
    onehot = (flat_routes[:, None] == jnp.arange(experts, dtype=jnp.int32)[None, :]).astype(
        jnp.int32
    )
    earlier = jnp.cumsum(onehot, axis=0) - onehot
    position = jnp.sum(earlier * onehot, axis=1)
    target = (flat_routes * capacity + position).reshape(tok_count, top_count)
    slot_ids = jnp.arange(experts * capacity, dtype=jnp.int32)
    hits = target[None, :, :] == slot_ids[:, None, None]
    matches = hits.astype(f32)
    select = jnp.sum(matches, axis=2)
    weighted = jnp.sum(matches * mix_rows[None, :, :], axis=2)
    return (target, select, weighted)


def per_device(tokens, routes, mix_weights, w_gate, w_up, w_down, upstream):
    experts = lax.axis_size("expert")
    section = lax.axis_index("section")
    my_x, my_z = section // NZ, section % NZ
    tok_count, feat = tokens.shape
    top_count = routes.shape[1]
    capacity = 5 * tok_count * top_count // (4 * experts)
    rows = experts * capacity
    ff = w_gate.shape[2]
    wide_x, wide_z = NX * feat, NZ * feat
    full = NX * wide_z
    where = my_x.reshape(1).astype(jnp.int32)
    gate4 = w_gate.reshape(NX, NZ, feat, ff)
    up4 = w_up.reshape(NX, NZ, feat, ff)
    down = w_down[0]

    tok_x = in_order([tokens] + [shift_x(tokens, d) for d in range(1, NX)], my_x, NX)
    tok_x, up_near = lax.optimization_barrier((tok_x, near_z(upstream)))
    up_pieces = far_z(up_near)
    target, select, weighted = slot_tables(routes, mix_weights, capacity, experts)
    slot_scale = jnp.sum(weighted, axis=1)
    select_low = select.astype(bf16)

    def exchange(value):
        return lax.all_to_all(
            value.reshape(experts, capacity, -1), "expert", split_axis=0, concat_axis=0, tiled=True
        ).reshape(rows, -1)

    tok_rows = exchange(jnp.dot(select_low, tok_x, preferred_element_type=f32).astype(bf16))
    tok_rows, up_pieces = lax.optimization_barrier((tok_rows, up_pieces))
    up_z = side_by_side(up_pieces, my_z)
    up_rows = jnp.dot(select_low, up_z, preferred_element_type=f32) * slot_scale[:, None]
    up_rows = exchange(up_rows.astype(bf16))

    dispatched = lax.all_gather(
        tok_rows, "section", axis_index_groups=Z_GROUPS, axis=1, tiled=True
    )
    ups = [up_rows] + [shift_x(up_rows, d) for d in range(1, NX)]

    def whole(*shape):
        return pl.BlockSpec(shape, lambda i, s: (0,) * len(shape))

    def clip(i, low, count):
        return jnp.clip(i - low, 0, count - 1)

    def weight_spec(low):
        return pl.BlockSpec((NX, 1, feat, ff), lambda i, s: (0, clip(i, low, NZ), 0, 0))

    def struct(shape, kind):
        return jax.ShapeDtypeStruct(shape, kind)

    tok_spec = pl.BlockSpec((rows, wide_x), lambda i, s: (0, clip(i, 0, NZ)))
    coef, silu_gate, hidden, *outs = call(
        forward_kernel,
        NZ + NX,
        [
            tok_spec,
            weight_spec(0),
            weight_spec(0),
            pl.BlockSpec((ff, wide_z), lambda i, s: (0, (s[0] + clip(i, NZ, NX)) % NX)),
        ],
        [whole(rows, ff)] * 3 + [whole(rows, wide_z)] * NX,
        [struct((rows, ff), f32)] * 2
        + [struct((rows, ff), bf16)]
        + [struct((rows, wide_z), bf16)] * NX,
        [pltpu.VMEM((rows, ff), f32)] * 2,
        6 * rows * full * ff,
        2 * (2 * rows * full + 3 * full * ff),
        (where, dispatched, gate4, up4, down),
    )

    sent_x = [shift_x(outs[d], d) for d in range(1, NX)]

    back, gate_act, up_act, mix_part = call(
        backward_kernel,
        NX + NZ,
        [whole(rows, wide_z)] * NX
        + [
            pl.BlockSpec((ff, wide_z), lambda i, s: (0, (s[0] + NX - clip(i, 0, NX)) % NX)),
            weight_spec(NX),
            weight_spec(NX),
        ]
        + [whole(rows, ff)] * 3,
        [pl.BlockSpec((1, rows, wide_x), lambda i, s: (clip(i, NX, NZ), 0, 0))]
        + [whole(rows, ff)] * 2
        + [whole(rows, 128)],
        [struct((NZ, rows, wide_x), bf16)]
        + [struct((rows, ff), bf16)] * 2
        + [struct((rows, 128), f32)],
        [pltpu.VMEM((rows, ff), f32)],
        0,
        0,
        (where, *ups, down, gate4, up4, coef, silu_gate, hidden),
    )

    back_z = lax.psum_scatter(
        back.reshape(NZ * rows, wide_x),
        "section",
        axis_index_groups=Z_GROUPS,
        scatter_dimension=0,
        tiled=True,
    )
    grad_gate, grad_up, grad_down = call(
        weight_kernel,
        NZ + NX,
        [tok_spec] + [whole(rows, ff)] * 3 + [whole(rows, wide_z)] * NX,
        [weight_spec(0)] * 2
        + [pl.BlockSpec((ff, wide_z), lambda i, s: (0, (s[0] + NX - clip(i, NZ, NX)) % NX))],
        [struct((NX, NZ, feat, ff), bf16)] * 2 + [struct((ff, full), bf16)],
        [],
        0,
        0,
        (where, dispatched, gate_act, up_act, hidden, *ups),
    )

    mix_sum = mix_part[:, 0].reshape(experts, capacity)

    sent_x, grads, mix_sum = lax.optimization_barrier(
        (sent_x, (grad_gate, grad_up, grad_down), mix_sum)
    )
    grad_gate, grad_up, grad_down = grads

    summed = outs[0].astype(f32)
    for term in sent_x:
        summed = summed + term.astype(f32)
    summed, mix_sum = lax.optimization_barrier((summed.astype(bf16), mix_sum))
    returned = exchange(summed).astype(f32)
    moe_out = jnp.dot(weighted.T, returned, precision=highest)
    mixed = (tokens.astype(f32) + spread_z(moe_out, my_z)).astype(bf16)

    for d in (2, 1):
        mix_sum = mix_sum + shift_x(mix_sum, d)
    for d in (4, 2, 1):
        mix_sum = mix_sum + shift_z(mix_sum, d)
    mix_rows = lax.all_to_all(mix_sum, "expert", split_axis=0, concat_axis=0, tiled=True)
    grad_mix = mix_rows.reshape(-1)[target] / mix_weights

    back_rows = exchange(back_z).astype(f32)
    grad_moe = jnp.dot(select.T, back_rows, precision=highest)
    grad_tokens = (upstream.astype(f32) + spread_x(grad_moe, my_x)).astype(bf16)
    return (
        mixed,
        grad_tokens,
        grad_mix,
        grad_gate.reshape(1, full, ff),
        grad_up.reshape(1, full, ff),
        grad_down[None],
    )


def solution(mesh):
    return jax.shard_map(
        per_device,
        mesh=mesh,
        in_specs=(
            P("expert", "section"),
            P("expert", None),
            P("expert", None),
            P("expert", None, "section"),
            P("expert", None, "section"),
            P("expert", "section", None),
            P("expert", "section"),
        ),
        out_specs=(
            P("expert", "section"),
            P("expert", "section"),
            P("expert", None),
            P("expert", None, "section"),
            P("expert", None, "section"),
            P("expert", "section", None),
        ),
        check_vma=False,
    )
```

```python
import functools

import jax
import jax.numpy as jnp
from jax import lax
from jax.experimental import pallas as pl
from jax.experimental.pallas import tpu as pltpu
from jax.sharding import PartitionSpec as P

highest = lax.Precision.HIGHEST
f32, bf16 = jnp.float32, jnp.bfloat16
NX, NZ = 4, 8
Z_GROUPS = [[x * NZ + z for z in range(NZ)] for x in range(NX)]


def shift_z(value, d):
    pairs = [(x * NZ + z, x * NZ + (z + d) % NZ) for x in range(NX) for z in range(NZ)]
    return lax.ppermute(value, "section", pairs)


def shift_x(value, d):
    pairs = [(x * NZ + z, ((x + d) % NX) * NZ + z) for x in range(NX) for z in range(NZ)]
    return lax.ppermute(value, "section", pairs)


def in_order(relative, own, count):
    held = jnp.stack(relative)
    return jnp.concatenate(
        [lax.dynamic_index_in_dim(held, (own - j) % count, 0, keepdims=False) for j in range(count)],
        axis=1,
    )


def spread_x(value, own):
    parts = value.reshape(value.shape[0], NX, -1).transpose(1, 0, 2)

    def part(d):
        return lax.dynamic_index_in_dim(parts, (own + d) % NX, 0, keepdims=False)

    sent = [shift_x(part(d).astype(bf16), d) for d in range(1, NX)]
    return sum((term.astype(f32) for term in sent), part(0))


def spread_z(value, own):
    parts = value.reshape(value.shape[0], NZ, -1).transpose(1, 0, 2)

    def part(d):
        return lax.dynamic_index_in_dim(parts, (own + d) % NZ, 0, keepdims=False)

    sent = [shift_z(part(d).astype(bf16), d) for d in (4, 3, -3, 2, -2, 1, -1)]
    return sum((term.astype(f32) for term in sent), part(0))


def ring_gather_x(value):
    half = value.shape[1] // 2
    a, b = value[:, :half], value[:, half:]
    below_a, above_b = shift_x(a, 1), shift_x(b, -1)
    below_b, above_a = shift_x(b, 1), shift_x(a, -1)
    far_a, far_b = shift_x(below_a, 1), shift_x(above_b, -1)
    return [(a, b), (below_a, below_b), (far_a, far_b), (above_a, above_b)]


def ring_scatter_x(parts):
    far_a, far_b = shift_x(parts[2][0], 1), shift_x(parts[2][1], -1)
    below_b, above_a = shift_x(parts[1][1], 1), shift_x(parts[3][0], -1)
    next_a = (parts[1][0].astype(f32) + far_a.astype(f32)).astype(bf16)
    next_b = (parts[3][1].astype(f32) + far_b.astype(f32)).astype(bf16)
    below_a, above_b = shift_x(next_a, 1), shift_x(next_b, -1)
    return [(below_a, below_b), (above_a, above_b)]


def near_z(value):
    return jnp.stack([shift_z(value, 1), value, shift_z(value, -1)])


def far_z(near):
    low, high = shift_z(near, 3), shift_z(near[:2], -3)
    return [low, near, high]


def side_by_side(pieces, own):
    held = jnp.concatenate(pieces)
    return jnp.concatenate(
        [
            lax.dynamic_index_in_dim(held, (j - own + 4) % NZ, 0, keepdims=False)
            for j in range(NZ)
        ],
        axis=1,
    )


def dot_nt(a, b):
    return lax.dot_general(a, b, (((1,), (1,)), ((), ())), preferred_element_type=f32)


def dot_tn(a, b):
    return lax.dot_general(a, b, (((0,), (0,)), ((), ())), preferred_element_type=f32)


def forward_kernel(
    x_ref, tok_ref, gate_ref, up_ref, down_ref, coef_ref, silu_ref, hid_ref, *rest
):
    outs, (acc_gate, acc_up) = rest[: 2 * NX], rest[2 * NX :]
    step = pl.program_id(0)
    width = gate_ref.shape[-1]

    @pl.when(step == 0)
    def _():
        acc_gate[...] = jnp.zeros_like(acc_gate)
        acc_up[...] = jnp.zeros_like(acc_up)

    @pl.when(step < NZ)
    def _():
        block = tok_ref[...]
        gate = gate_ref[...].reshape(-1, width)
        up = up_ref[...].reshape(-1, width)
        acc_gate[...] += jnp.dot(block, gate, preferred_element_type=f32)
        acc_up[...] += jnp.dot(block, up, preferred_element_type=f32)

    @pl.when(step == NZ - 1)
    def _():
        act_gate, act_up = acc_gate[...], acc_up[...]
        sig = jax.nn.sigmoid(act_gate)
        silu_gate = act_gate * sig
        silu_ref[...] = silu_gate
        coef_ref[...] = act_up * (sig * (1.0 + act_gate * (1.0 - sig)))
        hid_ref[...] = (silu_gate * act_up).astype(bf16)

    for d in range(NX):

        @pl.when(step == NZ + d)
        def _(d=d):
            half = down_ref.shape[1] // 2
            for h in range(2):
                outs[2 * d + h][...] = jnp.dot(
                    hid_ref[...],
                    down_ref[:, h * half : (h + 1) * half],
                    preferred_element_type=f32,
                ).astype(bf16)


def backward_kernel(x_ref, *refs):
    ups, refs = refs[: 2 * NX], refs[2 * NX :]
    down_ref, gate_ref, up_ref, coef_ref, silu_ref, hid_ref = refs[:6]
    part_ref, gate_out, up_out, mix_out, acc = refs[6:]
    step = pl.program_id(0)
    width = gate_ref.shape[-1]

    for d in range(NX):

        @pl.when(step == d)
        def _(d=d):
            half = down_ref.shape[1] // 2
            term = dot_nt(ups[2 * d][...], down_ref[:, :half])
            term += dot_nt(ups[2 * d + 1][...], down_ref[:, half:])
            acc[...] = term if d == 0 else acc[...] + term

    @pl.when(step == NX - 1)
    def _():
        grad_hidden = acc[...]
        gate_out[...] = (grad_hidden * coef_ref[...]).astype(bf16)
        up_out[...] = (grad_hidden * silu_ref[...]).astype(bf16)
        terms = jnp.sum(grad_hidden * hid_ref[...].astype(f32), axis=1, keepdims=True)
        mix_out[...] = jnp.broadcast_to(terms, mix_out.shape)

    @pl.when(step >= NX)
    def _():
        gate = gate_ref[...].reshape(-1, width)
        up = up_ref[...].reshape(-1, width)
        part_ref[0] = (dot_nt(gate_out[...], gate) + dot_nt(up_out[...], up)).astype(bf16)


def weight_kernel(x_ref, *refs):
    tok_ref, gact_ref, uact_ref, hid_ref = refs[:4]
    ups = refs[4 : 4 + 2 * NX]
    gate_out, up_out, down_out = refs[4 + 2 * NX :]
    step = pl.program_id(0)

    @pl.when(step < NZ)
    def _():
        block = tok_ref[...]
        gate_out[...] = dot_tn(block, gact_ref[...]).astype(bf16).reshape(gate_out.shape)
        up_out[...] = dot_tn(block, uact_ref[...]).astype(bf16).reshape(up_out.shape)

    for d in range(NX):

        @pl.when(step == NZ + d)
        def _(d=d):
            half = down_out.shape[1] // 2
            for h in range(2):
                down_out[:, h * half : (h + 1) * half] = dot_tn(
                    hid_ref[...], ups[2 * d + h][...]
                ).astype(bf16)


def call(kernel, steps, in_specs, out_specs, out_shape, scratch, flops, moved, args):
    return pl.pallas_call(
        kernel,
        grid_spec=pltpu.PrefetchScalarGridSpec(
            num_scalar_prefetch=1,
            grid=(steps,),
            in_specs=in_specs,
            out_specs=out_specs,
            scratch_shapes=scratch,
        ),
        out_shape=out_shape,
        compiler_params=pltpu.CompilerParams(vmem_limit_bytes=50 * 1024 * 1024),
        cost_estimate=pl.CostEstimate(flops=flops, bytes_accessed=moved, transcendentals=0),
    )(*args)


def slot_tables(route_rows, mix_rows, capacity, experts):
    tok_count, top_count = route_rows.shape
    flat_routes = route_rows.reshape(-1)
    onehot = (flat_routes[:, None] == jnp.arange(experts, dtype=jnp.int32)[None, :]).astype(
        jnp.int32
    )
    earlier = jnp.cumsum(onehot, axis=0) - onehot
    position = jnp.sum(earlier * onehot, axis=1)
    target = (flat_routes * capacity + position).reshape(tok_count, top_count)
    slot_ids = jnp.arange(experts * capacity, dtype=jnp.int32)
    hits = target[None, :, :] == slot_ids[:, None, None]
    matches = hits.astype(f32)
    select = jnp.sum(matches, axis=2)
    weighted = jnp.sum(matches * mix_rows[None, :, :], axis=2)
    return (target, select, weighted)


def per_device(tokens, routes, mix_weights, w_gate, w_up, w_down, upstream):
    experts = lax.axis_size("expert")
    section = lax.axis_index("section")
    my_x, my_z = section // NZ, section % NZ
    tok_count, feat = tokens.shape
    top_count = routes.shape[1]
    capacity = 5 * tok_count * top_count // (4 * experts)
    rows = experts * capacity
    ff = w_gate.shape[2]
    wide_x, wide_z = NX * feat, NZ * feat
    full = NX * wide_z
    where = my_x.reshape(1).astype(jnp.int32)
    gate4 = w_gate.reshape(NX, NZ, feat, ff)
    up4 = w_up.reshape(NX, NZ, feat, ff)
    down = w_down[0]

    up_near = near_z(upstream)
    target, select, weighted = slot_tables(routes, mix_weights, capacity, experts)
    slot_scale = jnp.sum(weighted, axis=1)
    select_low = select.astype(bf16)

    def exchange(value):
        return lax.all_to_all(
            value.reshape(experts, capacity, -1), "expert", split_axis=0, concat_axis=0, tiled=True
        ).reshape(rows, -1)

    tok_sent = jnp.dot(select_low, tokens, preferred_element_type=f32).astype(bf16)
    tok_sent, up_near = lax.optimization_barrier((tok_sent, up_near))
    up_pieces = far_z(up_near)
    tok_rows, up_pieces = lax.optimization_barrier((exchange(tok_sent), up_pieces))
    tok_x = in_order([tok_rows] + [shift_x(tok_rows, d) for d in range(1, NX)], my_x, NX)
    up_z = side_by_side(up_pieces, my_z)
    up_rows = jnp.dot(select_low, up_z, preferred_element_type=f32) * slot_scale[:, None]
    up_rows = exchange(up_rows.astype(bf16))

    dispatched = lax.all_gather(
        tok_x, "section", axis_index_groups=Z_GROUPS, axis=1, tiled=True
    )
    ups = [half for pair in ring_gather_x(up_rows) for half in pair]

    def whole(*shape):
        return pl.BlockSpec(shape, lambda i, s: (0,) * len(shape))

    def clip(i, low, count):
        return jnp.clip(i - low, 0, count - 1)

    def weight_spec(low):
        return pl.BlockSpec((NX, 1, feat, ff), lambda i, s: (0, clip(i, low, NZ), 0, 0))

    def struct(shape, kind):
        return jax.ShapeDtypeStruct(shape, kind)

    tok_spec = pl.BlockSpec((rows, wide_x), lambda i, s: (0, clip(i, 0, NZ)))
    coef, silu_gate, hidden, *outs = call(
        forward_kernel,
        NZ + NX,
        [
            tok_spec,
            weight_spec(0),
            weight_spec(0),
            pl.BlockSpec((ff, wide_z), lambda i, s: (0, (s[0] + clip(i, NZ, NX)) % NX)),
        ],
        [whole(rows, ff)] * 3 + [whole(rows, wide_z // 2)] * (2 * NX),
        [struct((rows, ff), f32)] * 2
        + [struct((rows, ff), bf16)]
        + [struct((rows, wide_z // 2), bf16)] * (2 * NX),
        [pltpu.VMEM((rows, ff), f32)] * 2,
        6 * rows * full * ff,
        2 * (2 * rows * full + 3 * full * ff),
        (where, dispatched, gate4, up4, down),
    )

    sent_x = ring_scatter_x([(outs[2 * d], outs[2 * d + 1]) for d in range(NX)])

    back, gate_act, up_act, mix_part = call(
        backward_kernel,
        NX + NZ,
        [whole(rows, wide_z // 2)] * (2 * NX)
        + [
            pl.BlockSpec((ff, wide_z), lambda i, s: (0, (s[0] + NX - clip(i, 0, NX)) % NX)),
            weight_spec(NX),
            weight_spec(NX),
        ]
        + [whole(rows, ff)] * 3,
        [pl.BlockSpec((1, rows, wide_x), lambda i, s: (clip(i, NX, NZ), 0, 0))]
        + [whole(rows, ff)] * 2
        + [whole(rows, 128)],
        [struct((NZ, rows, wide_x), bf16)]
        + [struct((rows, ff), bf16)] * 2
        + [struct((rows, 128), f32)],
        [pltpu.VMEM((rows, ff), f32)],
        0,
        0,
        (where, *ups, down, gate4, up4, coef, silu_gate, hidden),
    )

    back_z = lax.psum_scatter(
        back.reshape(NZ * rows, wide_x),
        "section",
        axis_index_groups=Z_GROUPS,
        scatter_dimension=0,
        tiled=True,
    )
    grad_gate, grad_up, grad_down = call(
        weight_kernel,
        NZ + NX,
        [tok_spec] + [whole(rows, ff)] * 3 + [whole(rows, wide_z // 2)] * (2 * NX),
        [weight_spec(0)] * 2
        + [pl.BlockSpec((ff, wide_z), lambda i, s: (0, (s[0] + NX - clip(i, NZ, NX)) % NX))],
        [struct((NX, NZ, feat, ff), bf16)] * 2 + [struct((ff, full), bf16)],
        [],
        0,
        0,
        (where, dispatched, gate_act, up_act, hidden, *ups),
    )

    mix_rows = lax.all_to_all(
        mix_part[:, 0].reshape(experts, capacity), "expert", split_axis=0, concat_axis=0, tiled=True
    )
    mix_sum = mix_rows.reshape(-1)[target].T / mix_weights.T
    for d in (4, 2, 1):
        mix_sum = mix_sum + shift_z(mix_sum, d)

    sent_x, grads, mix_sum = lax.optimization_barrier(
        (sent_x, (grad_gate, grad_up, grad_down), mix_sum)
    )
    grad_gate, grad_up, grad_down = grads

    summed = jnp.concatenate(
        [
            (outs[h].astype(f32) + sent_x[0][h].astype(f32) + sent_x[1][h].astype(f32)).astype(bf16)
            for h in range(2)
        ],
        axis=1,
    )
    returned, mix_sum = lax.optimization_barrier((exchange(summed), mix_sum))
    for d in (2, 1):
        mix_sum = mix_sum + shift_x(mix_sum, d)
    grad_mix = mix_sum.T
    returned, back_rows, grad_mix = lax.optimization_barrier((returned, exchange(back_z), grad_mix))

    moe_out = jnp.dot(weighted.T, returned.astype(f32), precision=highest)
    mixed = (tokens.astype(f32) + spread_z(moe_out, my_z)).astype(bf16)
    grad_moe = dot_tn(select_low, back_rows)
    grad_tokens = (upstream.astype(f32) + spread_x(grad_moe, my_x)).astype(bf16)
    return (
        mixed,
        grad_tokens,
        grad_mix,
        grad_gate.reshape(1, full, ff),
        grad_up.reshape(1, full, ff),
        grad_down[None],
    )


def solution(mesh):
    return jax.shard_map(
        per_device,
        mesh=mesh,
        in_specs=(
            P("expert", "section"),
            P("expert", None),
            P("expert", None),
            P("expert", None, "section"),
            P("expert", None, "section"),
            P("expert", "section", None),
            P("expert", "section"),
        ),
        out_specs=(
            P("expert", "section"),
            P("expert", "section"),
            P("expert", None),
            P("expert", None, "section"),
            P("expert", None, "section"),
            P("expert", "section", None),
        ),
        check_vma=False,
    )
```

```python
import functools

import jax
import jax.numpy as jnp
from jax import lax
from jax.experimental import pallas as pl
from jax.experimental.pallas import tpu as pltpu
from jax.sharding import PartitionSpec as P

highest = lax.Precision.HIGHEST
f32, bf16 = jnp.float32, jnp.bfloat16
NX, NZ = 4, 8
Z_GROUPS = [[x * NZ + z for z in range(NZ)] for x in range(NX)]


def shift_z(value, d):
    pairs = [(x * NZ + z, x * NZ + (z + d) % NZ) for x in range(NX) for z in range(NZ)]
    return lax.ppermute(value, "section", pairs)


def shift_x(value, d):
    pairs = [(x * NZ + z, ((x + d) % NX) * NZ + z) for x in range(NX) for z in range(NZ)]
    return lax.ppermute(value, "section", pairs)


def in_order(relative, own, count):
    held = jnp.stack(relative)
    return jnp.concatenate(
        [lax.dynamic_index_in_dim(held, (own - j) % count, 0, keepdims=False) for j in range(count)],
        axis=1,
    )


def spread_x(value, extra, own):
    parts = value.reshape(value.shape[0], NX, -1).transpose(1, 0, 2)

    def part(d):
        return lax.dynamic_index_in_dim(parts, (own + d) % NX, 0, keepdims=False)

    sent = [
        shift_x(jnp.concatenate([part(d).astype(bf16), extra]), d).astype(f32) for d in range(1, NX)
    ]
    total = sum(sent, jnp.concatenate([part(0), extra.astype(f32)]))
    return total[: value.shape[0]], total[value.shape[0] :]


def high_low(value):
    high = value.astype(bf16)
    return high, (value - high.astype(f32)).astype(bf16)


def spread_z(value, own):
    parts = value.reshape(value.shape[0], NZ, -1).transpose(1, 0, 2)

    def part(d):
        return lax.dynamic_index_in_dim(parts, (own + d) % NZ, 0, keepdims=False)

    sent = [shift_z(part(d).astype(bf16), d) for d in (4, 3, -3, 2, -2, 1, -1)]
    return sum((term.astype(f32) for term in sent), part(0))


def ring_gather_x(value):
    half = value.shape[1] // 2
    a, b = value[:, :half], value[:, half:]
    below_a, above_b = shift_x(a, 1), shift_x(b, -1)
    below_b, above_a = shift_x(b, 1), shift_x(a, -1)
    far_a, far_b = shift_x(below_a, 1), shift_x(above_b, -1)
    return [(a, b), (below_a, below_b), (far_a, far_b), (above_a, above_b)]


def ring_scatter_x(parts):
    far_a, far_b = shift_x(parts[2][0], 1), shift_x(parts[2][1], -1)
    below_b, above_a = shift_x(parts[1][1], 1), shift_x(parts[3][0], -1)
    next_a = (parts[1][0].astype(f32) + far_a.astype(f32)).astype(bf16)
    next_b = (parts[3][1].astype(f32) + far_b.astype(f32)).astype(bf16)
    below_a, above_b = shift_x(next_a, 1), shift_x(next_b, -1)
    return [(below_a, below_b), (above_a, above_b)]


def near_z(value):
    return jnp.stack([shift_z(value, 1), value, shift_z(value, -1)])


def far_z(near):
    low, high = shift_z(near, 3), shift_z(near[:2], -3)
    return [low, near, high]


def side_by_side(pieces, own):
    held = jnp.concatenate(pieces)
    return jnp.concatenate(
        [
            lax.dynamic_index_in_dim(held, (j - own + 4) % NZ, 0, keepdims=False)
            for j in range(NZ)
        ],
        axis=1,
    )


def dot_nt(a, b):
    return lax.dot_general(a, b, (((1,), (1,)), ((), ())), preferred_element_type=f32)


def dot_tn(a, b):
    return lax.dot_general(a, b, (((0,), (0,)), ((), ())), preferred_element_type=f32)


def forward_kernel(
    x_ref, tok_ref, gate_ref, up_ref, down_ref, coef_ref, silu_ref, hid_ref, *rest
):
    outs, (acc_gate, acc_up, made) = rest[: 2 * NX], rest[2 * NX :]
    step = pl.program_id(0)
    width = gate_ref.shape[-1]

    @pl.when(step == 0)
    def _():
        acc_gate[...] = jnp.zeros_like(acc_gate)
        acc_up[...] = jnp.zeros_like(acc_up)

    @pl.when(step < NZ)
    def _():
        block = tok_ref[...]
        gate = gate_ref[...].reshape(-1, width)
        up = up_ref[...].reshape(-1, width)
        acc_gate[...] += jnp.dot(block, gate, preferred_element_type=f32)
        acc_up[...] += jnp.dot(block, up, preferred_element_type=f32)

    @pl.when(step == NZ - 1)
    def _():
        act_gate, act_up = acc_gate[...], acc_up[...]
        sig = jax.nn.sigmoid(act_gate)
        silu_gate = act_gate * sig
        silu_ref[...] = silu_gate
        coef_ref[...] = act_up * (sig * (1.0 + act_gate * (1.0 - sig)))
        hid_ref[...] = (silu_gate * act_up).astype(bf16)

    @pl.when(step >= NZ)
    def _():
        made[...] = jnp.dot(hid_ref[...], down_ref[...], preferred_element_type=f32).astype(bf16)

    for d in range(NX):

        @pl.when(step == NZ + d)
        def _(d=d):
            half = made.shape[1] // 2
            outs[2 * d][...] = made[:, :half]
            outs[2 * d + 1][...] = made[:, half:]


def backward_kernel(x_ref, *refs):
    ups, refs = refs[: 2 * NX], refs[2 * NX :]
    down_ref, gate_ref, up_ref, coef_ref, silu_ref, hid_ref = refs[:6]
    part_ref, gate_out, up_out, acc, piece, mix = refs[6:]
    step = pl.program_id(0)
    width = gate_ref.shape[-1]
    rows = acc.shape[0]

    for d in range(NX):

        @pl.when(step == d)
        def _(d=d):
            half = piece.shape[1] // 2
            piece[:, :half] = ups[2 * d][...]
            piece[:, half:] = ups[2 * d + 1][...]

    @pl.when(step == 0)
    def _():
        acc[...] = jnp.zeros_like(acc)

    @pl.when(step < NX)
    def _():
        acc[...] += dot_nt(piece[...], down_ref[...])

    @pl.when(step == NX - 1)
    def _():
        grad_hidden = acc[...]
        gate_out[...] = (grad_hidden * coef_ref[...]).astype(bf16)
        up_out[...] = (grad_hidden * silu_ref[...]).astype(bf16)
        terms = grad_hidden * hid_ref[...].astype(f32)
        sums = lax.dot_general(
            jnp.ones((8, width), f32),
            terms,
            (((1,), (1,)), ((), ())),
            precision=highest,
            preferred_element_type=f32,
        )
        high, low = high_low(sums)
        cut = part_ref.shape[2]
        tail = jnp.zeros((1, 2 * cut - rows), bf16)
        mix[...] = jnp.concatenate(
            [
                high[:1, :cut],
                jnp.concatenate([high[:1, cut:], tail], axis=1),
                low[:1, :cut],
                jnp.concatenate([low[:1, cut:], tail], axis=1),
                jnp.zeros((4, cut), bf16),
            ]
        )

    @pl.when(step >= NX)
    def _():
        gate = gate_ref[...].reshape(-1, width)
        up = up_ref[...].reshape(-1, width)
        part_ref[0, :rows] = (dot_nt(gate_out[...], gate) + dot_nt(up_out[...], up)).astype(bf16)
        part_ref[0, rows:] = mix[...]


def weight_kernel(x_ref, *refs):
    tok_ref, gact_ref, uact_ref, hid_ref = refs[:4]
    ups = refs[4 : 4 + 2 * NX]
    gate_out, up_out, down_out, piece = refs[4 + 2 * NX :]
    step = pl.program_id(0)

    @pl.when(step < NZ)
    def _():
        block = tok_ref[...]
        gate_out[...] = dot_tn(block, gact_ref[...]).astype(bf16).reshape(gate_out.shape)
        up_out[...] = dot_tn(block, uact_ref[...]).astype(bf16).reshape(up_out.shape)

    for d in range(NX):

        @pl.when(step == NZ + d)
        def _(d=d):
            half = piece.shape[1] // 2
            piece[:, :half] = ups[2 * d][...]
            piece[:, half:] = ups[2 * d + 1][...]

    @pl.when(step >= NZ)
    def _():
        down_out[...] = dot_tn(hid_ref[...], piece[...]).astype(bf16)


def call(kernel, steps, in_specs, out_specs, out_shape, scratch, flops, moved, args):
    return pl.pallas_call(
        kernel,
        grid_spec=pltpu.PrefetchScalarGridSpec(
            num_scalar_prefetch=1,
            grid=(steps,),
            in_specs=in_specs,
            out_specs=out_specs,
            scratch_shapes=scratch,
        ),
        out_shape=out_shape,
        compiler_params=pltpu.CompilerParams(vmem_limit_bytes=50 * 1024 * 1024),
        cost_estimate=pl.CostEstimate(flops=flops, bytes_accessed=moved, transcendentals=0),
    )(*args)


def slot_tables(route_rows, mix_rows, capacity, experts):
    tok_count, top_count = route_rows.shape
    flat_routes = route_rows.reshape(-1)
    onehot = (flat_routes[:, None] == jnp.arange(experts, dtype=jnp.int32)[None, :]).astype(
        jnp.int32
    )
    earlier = jnp.cumsum(onehot, axis=0) - onehot
    position = jnp.sum(earlier * onehot, axis=1)
    target = (flat_routes * capacity + position).reshape(tok_count, top_count)
    slot_ids = jnp.arange(experts * capacity, dtype=jnp.int32)
    hits = target[None, :, :] == slot_ids[:, None, None]
    matches = hits.astype(f32)
    select = jnp.sum(matches, axis=2)
    weighted = jnp.sum(matches * mix_rows[None, :, :], axis=2)
    return (target, select, weighted)


def per_device(tokens, routes, mix_weights, w_gate, w_up, w_down, upstream):
    experts = lax.axis_size("expert")
    section = lax.axis_index("section")
    my_x, my_z = section // NZ, section % NZ
    tok_count, feat = tokens.shape
    top_count = routes.shape[1]
    capacity = 5 * tok_count * top_count // (4 * experts)
    rows = experts * capacity
    ff = w_gate.shape[2]
    wide_x, wide_z = NX * feat, NZ * feat
    full = NX * wide_z
    where = my_x.reshape(1).astype(jnp.int32)
    gate4 = w_gate.reshape(NX, NZ, feat, ff)
    up4 = w_up.reshape(NX, NZ, feat, ff)
    down = w_down[0]

    up_near = near_z(upstream)
    target, select, weighted = slot_tables(routes, mix_weights, capacity, experts)
    slot_scale = jnp.sum(weighted, axis=1)
    select_low = select.astype(bf16)

    def exchange(value):
        return lax.all_to_all(
            value.reshape(experts, -1, value.shape[-1]), "expert", split_axis=0, concat_axis=0, tiled=True
        ).reshape(-1, value.shape[-1])

    tok_sent = jnp.dot(select_low, tokens, preferred_element_type=f32).astype(bf16)
    tok_sent, up_near = lax.optimization_barrier((tok_sent, up_near))
    up_pieces = far_z(up_near)
    tok_rows, up_pieces = lax.optimization_barrier((exchange(tok_sent), up_pieces))
    tok_x = in_order([tok_rows] + [shift_x(tok_rows, d) for d in range(1, NX)], my_x, NX)
    up_z = side_by_side(up_pieces, my_z)
    up_rows = jnp.dot(select_low, up_z, preferred_element_type=f32) * slot_scale[:, None]
    up_rows = exchange(up_rows.astype(bf16))

    dispatched = lax.all_gather(
        tok_x, "section", axis_index_groups=Z_GROUPS, axis=1, tiled=True
    )
    ups = [half for pair in ring_gather_x(up_rows) for half in pair]

    def whole(*shape):
        return pl.BlockSpec(shape, lambda i, s: (0,) * len(shape))

    def clip(i, low, count):
        return jnp.clip(i - low, 0, count - 1)

    def weight_spec(low):
        return pl.BlockSpec((NX, 1, feat, ff), lambda i, s: (0, clip(i, low, NZ), 0, 0))

    def struct(shape, kind):
        return jax.ShapeDtypeStruct(shape, kind)

    tok_spec = pl.BlockSpec((rows, wide_x), lambda i, s: (0, clip(i, 0, NZ)))
    coef, silu_gate, hidden, *outs = call(
        forward_kernel,
        NZ + NX,
        [
            tok_spec,
            weight_spec(0),
            weight_spec(0),
            pl.BlockSpec((ff, wide_z), lambda i, s: (0, (s[0] + clip(i, NZ, NX)) % NX)),
        ],
        [whole(rows, ff)] * 3 + [whole(rows, wide_z // 2)] * (2 * NX),
        [struct((rows, ff), f32)] * 2
        + [struct((rows, ff), bf16)]
        + [struct((rows, wide_z // 2), bf16)] * (2 * NX),
        [pltpu.VMEM((rows, ff), f32)] * 2 + [pltpu.VMEM((rows, wide_z), bf16)],
        6 * rows * full * ff,
        2 * (2 * rows * full + 3 * full * ff),
        (where, dispatched, gate4, up4, down),
    )

    sent_x = ring_scatter_x([(outs[2 * d], outs[2 * d + 1]) for d in range(NX)])

    back, gate_act, up_act = call(
        backward_kernel,
        NX + NZ,
        [whole(rows, wide_z // 2)] * (2 * NX)
        + [
            pl.BlockSpec((ff, wide_z), lambda i, s: (0, (s[0] + NX - clip(i, 0, NX)) % NX)),
            weight_spec(NX),
            weight_spec(NX),
        ]
        + [whole(rows, ff)] * 3,
        [pl.BlockSpec((1, rows + 8, wide_x), lambda i, s: (clip(i, NX, NZ), 0, 0))]
        + [whole(rows, ff)] * 2,
        [struct((NZ, rows + 8, wide_x), bf16)] + [struct((rows, ff), bf16)] * 2,
        [
            pltpu.VMEM((rows, ff), f32),
            pltpu.VMEM((rows, wide_z), bf16),
            pltpu.VMEM((8, wide_x), bf16),
        ],
        0,
        0,
        (where, *ups, down, gate4, up4, coef, silu_gate, hidden),
    )

    back_z = lax.psum_scatter(
        back.reshape(NZ * (rows + 8), wide_x),
        "section",
        axis_index_groups=Z_GROUPS,
        scatter_dimension=0,
        tiled=True,
    )
    grad_gate, grad_up, grad_down = call(
        weight_kernel,
        NZ + NX,
        [tok_spec] + [whole(rows, ff)] * 3 + [whole(rows, wide_z // 2)] * (2 * NX),
        [weight_spec(0)] * 2
        + [pl.BlockSpec((ff, wide_z), lambda i, s: (0, (s[0] + NX - clip(i, NZ, NX)) % NX))],
        [struct((NX, NZ, feat, ff), bf16)] * 2 + [struct((ff, full), bf16)],
        [pltpu.VMEM((rows, wide_z), bf16)],
        0,
        0,
        (where, dispatched, gate_act, up_act, hidden, *ups),
    )

    sent_x, grads = lax.optimization_barrier((sent_x, (grad_gate, grad_up, grad_down)))
    grad_gate, grad_up, grad_down = grads

    summed = jnp.concatenate(
        [
            (outs[h].astype(f32) + sent_x[0][h].astype(f32) + sent_x[1][h].astype(f32)).astype(bf16)
            for h in range(2)
        ],
        axis=1,
    )
    returned = exchange(summed)

    mix = back_z[rows : rows + 4].reshape(2, 2 * wide_x)[:, :rows].reshape(2, experts, capacity)
    mix = jnp.pad(mix.transpose(1, 0, 2), ((0, 0), (0, 6), (0, wide_x - capacity)))
    back = exchange(
        jnp.concatenate([back_z[:rows].reshape(experts, capacity, wide_x), mix], axis=1)
    ).reshape(experts, capacity + 8, wide_x)
    returned, back = lax.optimization_barrier((returned, back))

    moe_out = jnp.dot(weighted.T, returned.astype(f32), precision=highest)
    mixed = (tokens.astype(f32) + spread_z(moe_out, my_z)).astype(bf16)
    grad_moe = dot_tn(select_low, back[:, :capacity].reshape(rows, wide_x))
    mix = jnp.sum(back[:, capacity : capacity + 2, :capacity].astype(f32), axis=1)
    mix = mix.reshape(-1)[target.T].reshape(-1, feat)
    grad_moe, mix = spread_x(grad_moe, jnp.concatenate(high_low(mix)), my_x)
    grad_tokens = (upstream.astype(f32) + grad_moe).astype(bf16)
    mix = jnp.sum(mix.reshape(2, top_count, tok_count), axis=0)
    grad_mix = mix.T / mix_weights
    return (
        mixed,
        grad_tokens,
        grad_mix,
        grad_gate.reshape(1, full, ff),
        grad_up.reshape(1, full, ff),
        grad_down[None],
    )


def solution(mesh):
    return jax.shard_map(
        per_device,
        mesh=mesh,
        in_specs=(
            P("expert", "section"),
            P("expert", None),
            P("expert", None),
            P("expert", None, "section"),
            P("expert", None, "section"),
            P("expert", "section", None),
            P("expert", "section"),
        ),
        out_specs=(
            P("expert", "section"),
            P("expert", "section"),
            P("expert", None),
            P("expert", None, "section"),
            P("expert", None, "section"),
            P("expert", "section", None),
        ),
        check_vma=False,
    )
```

```python
import functools

import jax
import jax.numpy as jnp
from jax import lax
from jax.experimental import pallas as pl
from jax.experimental.pallas import tpu as pltpu
from jax.sharding import PartitionSpec as P

highest = lax.Precision.HIGHEST
f32, bf16 = jnp.float32, jnp.bfloat16
NX, NZ = 4, 8
Z_GROUPS = [[x * NZ + z for z in range(NZ)] for x in range(NX)]


def shift_z(value, d):
    pairs = [(x * NZ + z, x * NZ + (z + d) % NZ) for x in range(NX) for z in range(NZ)]
    return lax.ppermute(value, "section", pairs)


def shift_x(value, d):
    pairs = [(x * NZ + z, ((x + d) % NX) * NZ + z) for x in range(NX) for z in range(NZ)]
    return lax.ppermute(value, "section", pairs)


def in_order(relative, own, count):
    held = jnp.stack(relative)
    return jnp.concatenate(
        [lax.dynamic_index_in_dim(held, (own - j) % count, 0, keepdims=False) for j in range(count)],
        axis=1,
    )


def spread_x(value, extra, own):
    parts = value.reshape(value.shape[0], NX, -1).transpose(1, 0, 2)

    def part(d):
        return lax.dynamic_index_in_dim(parts, (own + d) % NX, 0, keepdims=False)

    sent = [
        shift_x(jnp.concatenate([part(d).astype(bf16), extra]), d).astype(f32) for d in range(1, NX)
    ]
    total = sum(sent, jnp.concatenate([part(0), extra.astype(f32)]))
    return total[: value.shape[0]], total[value.shape[0] :]


def high_low(value):
    high = value.astype(bf16)
    return high, (value - high.astype(f32)).astype(bf16)


def spread_z(value, own):
    parts = value.reshape(value.shape[0], NZ, -1).transpose(1, 0, 2)

    def part(d):
        return lax.dynamic_index_in_dim(parts, (own + d) % NZ, 0, keepdims=False)

    sent = [shift_z(part(d).astype(bf16), d) for d in (4, 3, -3, 2, -2, 1, -1)]
    return sum((term.astype(f32) for term in sent), part(0))


def ring_gather_x(value):
    half = value.shape[1] // 2
    a, b = value[:, :half], value[:, half:]
    below_a, above_b = shift_x(a, 1), shift_x(b, -1)
    below_b, above_a = shift_x(b, 1), shift_x(a, -1)
    far_a, far_b = shift_x(below_a, 1), shift_x(above_b, -1)
    return [(a, b), (below_a, below_b), (far_a, far_b), (above_a, above_b)]


def ring_scatter_x(parts, far):
    far_a, far_b = far
    below_b, above_a = shift_x(parts[1][1], 1), shift_x(parts[3][0], -1)
    next_a = (parts[1][0].astype(f32) + far_a.astype(f32)).astype(bf16)
    next_b = (parts[3][1].astype(f32) + far_b.astype(f32)).astype(bf16)
    below_a, above_b = shift_x(next_a, 1), shift_x(next_b, -1)
    return [(below_a, below_b), (above_a, above_b)]


def near_z(value):
    return jnp.stack([shift_z(value, 1), value, shift_z(value, -1)])


def far_z(near):
    low, high = shift_z(near, 3), shift_z(near[:2], -3)
    return [low, near, high]


def side_by_side(pieces, own):
    held = jnp.concatenate(pieces)
    return jnp.concatenate(
        [
            lax.dynamic_index_in_dim(held, (j - own + 4) % NZ, 0, keepdims=False)
            for j in range(NZ)
        ],
        axis=1,
    )


def dot_nt(a, b):
    return lax.dot_general(a, b, (((1,), (1,)), ((), ())), preferred_element_type=f32)


def dot_tn(a, b):
    return lax.dot_general(a, b, (((0,), (0,)), ((), ())), preferred_element_type=f32)


def forward_kernel(
    x_ref, tok_ref, gate_ref, up_ref, down_ref, coef_ref, silu_ref, hid_ref, *rest
):
    outs, (acc_gate, acc_up, made) = rest[: 2 * NX], rest[2 * NX :]
    step = pl.program_id(0)
    width = gate_ref.shape[-1]

    @pl.when(step == 0)
    def _():
        acc_gate[...] = jnp.zeros_like(acc_gate)
        acc_up[...] = jnp.zeros_like(acc_up)

    @pl.when(step < NZ)
    def _():
        block = tok_ref[...]
        gate = gate_ref[...].reshape(-1, width)
        up = up_ref[...].reshape(-1, width)
        acc_gate[...] += jnp.dot(block, gate, preferred_element_type=f32)
        acc_up[...] += jnp.dot(block, up, preferred_element_type=f32)

    @pl.when(step == NZ - 1)
    def _():
        act_gate, act_up = acc_gate[...], acc_up[...]
        sig = jax.nn.sigmoid(act_gate)
        silu_gate = act_gate * sig
        silu_ref[...] = silu_gate
        coef_ref[...] = act_up * (sig * (1.0 + act_gate * (1.0 - sig)))
        hid_ref[...] = (silu_gate * act_up).astype(bf16)

    @pl.when(step >= NZ)
    def _():
        made[...] = jnp.dot(hid_ref[...], down_ref[...], preferred_element_type=f32).astype(bf16)

    for d in range(NX):

        @pl.when(step == NZ + d)
        def _(d=d):
            half = made.shape[1] // 2
            outs[2 * d][...] = made[:, :half]
            outs[2 * d + 1][...] = made[:, half:]


def backward_kernel(x_ref, *refs):
    ups, refs = refs[: 2 * NX], refs[2 * NX :]
    down_ref, gate_ref, up_ref, coef_ref, silu_ref, hid_ref = refs[:6]
    part_ref, gate_out, up_out, acc, piece, mix = refs[6:]
    step = pl.program_id(0)
    width = gate_ref.shape[-1]
    rows = acc.shape[0]

    for d in range(NX):

        @pl.when(step == d)
        def _(d=d):
            half = piece.shape[1] // 2
            piece[:, :half] = ups[2 * d][...]
            piece[:, half:] = ups[2 * d + 1][...]

    @pl.when(step == 0)
    def _():
        acc[...] = jnp.zeros_like(acc)

    @pl.when(step < NX)
    def _():
        acc[...] += dot_nt(piece[...], down_ref[...])

    @pl.when(step == NX - 1)
    def _():
        grad_hidden = acc[...]
        gate_out[...] = (grad_hidden * coef_ref[...]).astype(bf16)
        up_out[...] = (grad_hidden * silu_ref[...]).astype(bf16)
        terms = grad_hidden * hid_ref[...].astype(f32)
        sums = lax.dot_general(
            jnp.ones((8, width), f32),
            terms,
            (((1,), (1,)), ((), ())),
            precision=highest,
            preferred_element_type=f32,
        )
        high, low = high_low(sums)
        cut = part_ref.shape[2]
        tail = jnp.zeros((1, 2 * cut - rows), bf16)
        mix[...] = jnp.concatenate(
            [
                high[:1, :cut],
                jnp.concatenate([high[:1, cut:], tail], axis=1),
                low[:1, :cut],
                jnp.concatenate([low[:1, cut:], tail], axis=1),
                jnp.zeros((4, cut), bf16),
            ]
        )

    @pl.when(step >= NX)
    def _():
        gate = gate_ref[...].reshape(-1, width)
        up = up_ref[...].reshape(-1, width)
        part_ref[0, :rows] = (dot_nt(gate_out[...], gate) + dot_nt(up_out[...], up)).astype(bf16)
        part_ref[0, rows:] = mix[...]


def weight_kernel(x_ref, *refs):
    tok_ref, gact_ref, uact_ref, hid_ref = refs[:4]
    ups = refs[4 : 4 + 2 * NX]
    gate_out, up_out, down_out, piece = refs[4 + 2 * NX :]
    step = pl.program_id(0)

    @pl.when(step < NZ)
    def _():
        block = tok_ref[...]
        gate_out[...] = dot_tn(block, gact_ref[...]).astype(bf16).reshape(gate_out.shape)
        up_out[...] = dot_tn(block, uact_ref[...]).astype(bf16).reshape(up_out.shape)

    for d in range(NX):

        @pl.when(step == NZ + d)
        def _(d=d):
            half = piece.shape[1] // 2
            piece[:, :half] = ups[2 * d][...]
            piece[:, half:] = ups[2 * d + 1][...]

    @pl.when(step >= NZ)
    def _():
        down_out[...] = dot_tn(hid_ref[...], piece[...]).astype(bf16)


def call(kernel, steps, in_specs, out_specs, out_shape, scratch, flops, moved, args):
    return pl.pallas_call(
        kernel,
        grid_spec=pltpu.PrefetchScalarGridSpec(
            num_scalar_prefetch=1,
            grid=(steps,),
            in_specs=in_specs,
            out_specs=out_specs,
            scratch_shapes=scratch,
        ),
        out_shape=out_shape,
        compiler_params=pltpu.CompilerParams(vmem_limit_bytes=50 * 1024 * 1024),
        cost_estimate=pl.CostEstimate(flops=flops, bytes_accessed=moved, transcendentals=0),
    )(*args)


def slot_tables(route_rows, mix_rows, capacity, experts):
    tok_count, top_count = route_rows.shape
    flat_routes = route_rows.reshape(-1)
    onehot = flat_routes[:, None] == jnp.arange(experts, dtype=jnp.int32)[None, :]
    count = tok_count * top_count
    pairs = jnp.arange(count, dtype=jnp.int32)
    before = (pairs[None, :] < pairs[:, None]).astype(bf16)
    earlier = jnp.dot(before, onehot.astype(bf16), preferred_element_type=f32)
    position = jnp.sum(jnp.where(onehot, earlier, 0.0), axis=1).astype(jnp.int32)
    target = (flat_routes * capacity + position).reshape(tok_count, top_count)
    slot_ids = jnp.arange(experts * capacity, dtype=jnp.int32)
    hits = target.T[None, :, :] == slot_ids[:, None, None]
    matches = hits.astype(f32)
    select = jnp.sum(matches, axis=1)
    weighted = jnp.sum(matches * mix_rows.T[None, :, :], axis=1)
    picks = matches.astype(bf16).reshape(experts * capacity, -1)
    return (select.astype(bf16), weighted, picks)


def per_device(tokens, routes, mix_weights, w_gate, w_up, w_down, upstream):
    experts = lax.axis_size("expert")
    section = lax.axis_index("section")
    my_x, my_z = section // NZ, section % NZ
    tok_count, feat = tokens.shape
    top_count = routes.shape[1]
    capacity = 5 * tok_count * top_count // (4 * experts)
    rows = experts * capacity
    ff = w_gate.shape[2]
    wide_x, wide_z = NX * feat, NZ * feat
    full = NX * wide_z
    where = my_x.reshape(1).astype(jnp.int32)
    gate4 = w_gate.reshape(NX, NZ, feat, ff)
    up4 = w_up.reshape(NX, NZ, feat, ff)
    down = w_down[0]

    up_near = near_z(upstream)
    select_low, weighted, picks = slot_tables(routes, mix_weights, capacity, experts)
    slot_scale = jnp.sum(weighted, axis=1)

    def exchange(value):
        return lax.all_to_all(
            value.reshape(experts, -1, value.shape[-1]), "expert", split_axis=0, concat_axis=0, tiled=True
        ).reshape(-1, value.shape[-1])

    tok_sent = jnp.dot(select_low, tokens, preferred_element_type=f32).astype(bf16)
    tok_sent, up_near = lax.optimization_barrier((tok_sent, up_near))
    up_pieces = far_z(up_near)
    tok_rows, up_pieces = lax.optimization_barrier((exchange(tok_sent), up_pieces))
    tok_x = in_order([tok_rows] + [shift_x(tok_rows, d) for d in range(1, NX)], my_x, NX)
    up_z = side_by_side(up_pieces, my_z)
    up_rows = jnp.dot(select_low, up_z, preferred_element_type=f32) * slot_scale[:, None]
    up_rows = exchange(up_rows.astype(bf16))

    dispatched = lax.all_gather(
        tok_x, "section", axis_index_groups=Z_GROUPS, axis=1, tiled=True
    )
    ups = [half for pair in ring_gather_x(up_rows) for half in pair]

    def whole(*shape):
        return pl.BlockSpec(shape, lambda i, s: (0,) * len(shape))

    def clip(i, low, count):
        return jnp.clip(i - low, 0, count - 1)

    def weight_spec(low):
        return pl.BlockSpec((NX, 1, feat, ff), lambda i, s: (0, clip(i, low, NZ), 0, 0))

    def struct(shape, kind):
        return jax.ShapeDtypeStruct(shape, kind)

    tok_spec = pl.BlockSpec((rows, wide_x), lambda i, s: (0, clip(i, 0, NZ)))
    coef, silu_gate, hidden, *outs = call(
        forward_kernel,
        NZ + NX,
        [
            tok_spec,
            weight_spec(0),
            weight_spec(0),
            pl.BlockSpec((ff, wide_z), lambda i, s: (0, (s[0] + clip(i, NZ, NX)) % NX)),
        ],
        [whole(rows, ff)] * 3 + [whole(rows, wide_z // 2)] * (2 * NX),
        [struct((rows, ff), f32)] * 2
        + [struct((rows, ff), bf16)]
        + [struct((rows, wide_z // 2), bf16)] * (2 * NX),
        [pltpu.VMEM((rows, ff), f32)] * 2 + [pltpu.VMEM((rows, wide_z), bf16)],
        6 * rows * full * ff,
        2 * (2 * rows * full + 3 * full * ff),
        (where, dispatched, gate4, up4, down),
    )

    outs = [(outs[2 * d], outs[2 * d + 1]) for d in range(NX)]
    far = shift_x(outs[2][0], 1), shift_x(outs[2][1], -1)

    back, gate_act, up_act = call(
        backward_kernel,
        NX + NZ,
        [whole(rows, wide_z // 2)] * (2 * NX)
        + [
            pl.BlockSpec((ff, wide_z), lambda i, s: (0, (s[0] + NX - clip(i, 0, NX)) % NX)),
            weight_spec(NX),
            weight_spec(NX),
        ]
        + [whole(rows, ff)] * 3,
        [pl.BlockSpec((1, rows + 8, wide_x), lambda i, s: (clip(i, NX, NZ), 0, 0))]
        + [whole(rows, ff)] * 2,
        [struct((NZ, rows + 8, wide_x), bf16)] + [struct((rows, ff), bf16)] * 2,
        [
            pltpu.VMEM((rows, ff), f32),
            pltpu.VMEM((rows, wide_z), bf16),
            pltpu.VMEM((8, wide_x), bf16),
        ],
        0,
        0,
        (where, *ups, down, gate4, up4, coef, silu_gate, hidden),
    )

    back, far = lax.optimization_barrier((back, far))
    sent_x = ring_scatter_x(outs, far)

    back_z = lax.psum_scatter(
        back.reshape(NZ * (rows + 8), wide_x),
        "section",
        axis_index_groups=Z_GROUPS,
        scatter_dimension=0,
        tiled=True,
    )
    grad_gate, grad_up, grad_down = call(
        weight_kernel,
        NZ + NX,
        [tok_spec] + [whole(rows, ff)] * 3 + [whole(rows, wide_z // 2)] * (2 * NX),
        [weight_spec(0)] * 2
        + [pl.BlockSpec((ff, wide_z), lambda i, s: (0, (s[0] + NX - clip(i, NZ, NX)) % NX))],
        [struct((NX, NZ, feat, ff), bf16)] * 2 + [struct((ff, full), bf16)],
        [pltpu.VMEM((rows, wide_z), bf16)],
        0,
        0,
        (where, dispatched, gate_act, up_act, hidden, *ups),
    )

    sent_x, grads = lax.optimization_barrier((sent_x, (grad_gate, grad_up, grad_down)))
    grad_gate, grad_up, grad_down = grads

    summed = jnp.concatenate(
        [
            (outs[0][h].astype(f32) + sent_x[0][h].astype(f32) + sent_x[1][h].astype(f32)).astype(bf16)
            for h in range(2)
        ],
        axis=1,
    )
    returned = exchange(summed)

    mix = back_z[rows : rows + 4].reshape(2, 2 * wide_x)[:, :rows].reshape(2, experts, capacity)
    mix = jnp.pad(mix.transpose(1, 0, 2), ((0, 0), (0, 6), (0, wide_x - capacity)))
    back = exchange(
        jnp.concatenate([back_z[:rows].reshape(experts, capacity, wide_x), mix], axis=1)
    ).reshape(experts, capacity + 8, wide_x)
    moe_out = jnp.dot(weighted.T, returned.astype(f32), precision=highest)
    mixed = (tokens.astype(f32) + spread_z(moe_out, my_z)).astype(bf16)
    mixed, back = lax.optimization_barrier((mixed, back))

    grad_moe = dot_tn(select_low, back[:, :capacity].reshape(rows, wide_x))
    mix = back[:, capacity : capacity + 2, :capacity].transpose(1, 0, 2).reshape(2, rows)
    mix = jnp.sum(jnp.dot(mix, picks, preferred_element_type=f32), axis=0).reshape(-1, feat)
    grad_moe, mix = spread_x(grad_moe, jnp.concatenate(high_low(mix)), my_x)
    grad_tokens = (upstream.astype(f32) + grad_moe).astype(bf16)
    mix = jnp.sum(mix.reshape(2, top_count, tok_count), axis=0)
    grad_mix = mix.T / mix_weights
    return (
        mixed,
        grad_tokens,
        grad_mix,
        grad_gate.reshape(1, full, ff),
        grad_up.reshape(1, full, ff),
        grad_down[None],
    )


def solution(mesh):
    return jax.shard_map(
        per_device,
        mesh=mesh,
        in_specs=(
            P("expert", "section"),
            P("expert", None),
            P("expert", None),
            P("expert", None, "section"),
            P("expert", None, "section"),
            P("expert", "section", None),
            P("expert", "section"),
        ),
        out_specs=(
            P("expert", "section"),
            P("expert", "section"),
            P("expert", None),
            P("expert", None, "section"),
            P("expert", None, "section"),
            P("expert", "section", None),
        ),
        check_vma=False,
    )
```

```python
import functools

import jax
import jax.numpy as jnp
from jax import lax
from jax.experimental import pallas as pl
from jax.experimental.pallas import tpu as pltpu
from jax.sharding import PartitionSpec as P

highest = lax.Precision.HIGHEST
f32, bf16 = jnp.float32, jnp.bfloat16
NX, NZ = 4, 8
Z_GROUPS = [[x * NZ + z for z in range(NZ)] for x in range(NX)]


def shift_z(value, d):
    pairs = [(x * NZ + z, x * NZ + (z + d) % NZ) for x in range(NX) for z in range(NZ)]
    return lax.ppermute(value, "section", pairs)


def shift_x(value, d):
    pairs = [(x * NZ + z, ((x + d) % NX) * NZ + z) for x in range(NX) for z in range(NZ)]
    return lax.ppermute(value, "section", pairs)


def in_order(relative, own, count):
    held = jnp.stack(relative)
    return jnp.concatenate(
        [lax.dynamic_index_in_dim(held, (own - j) % count, 0, keepdims=False) for j in range(count)],
        axis=1,
    )


def spread_x(value, extra, own):
    parts = value.reshape(value.shape[0], NX, -1).transpose(1, 0, 2)

    def part(d):
        return lax.dynamic_index_in_dim(parts, (own + d) % NX, 0, keepdims=False)

    sent = [
        shift_x(jnp.concatenate([part(d).astype(bf16), extra]), d).astype(f32) for d in range(1, NX)
    ]
    total = sum(sent, jnp.concatenate([part(0), extra.astype(f32)]))
    return total[: value.shape[0]], total[value.shape[0] :]


def high_low(value):
    high = value.astype(bf16)
    return high, (value - high.astype(f32)).astype(bf16)


def spread_z(value, own):
    parts = value.reshape(value.shape[0], NZ, -1).transpose(1, 0, 2)

    def part(d):
        return lax.dynamic_index_in_dim(parts, (own + d) % NZ, 0, keepdims=False)

    above = shift_z(jnp.stack([part(2), part(3), part(4)]).astype(bf16), 3).astype(f32)
    below = shift_z(jnp.stack([part(-3), part(-2)]).astype(bf16), -3).astype(f32)
    right = shift_z((part(1) + above[2] + below[1]).astype(bf16), 1)
    left = shift_z((part(-1) + above[0]).astype(bf16), -1)
    return part(0) + above[1] + below[0] + right.astype(f32) + left.astype(f32)


def ring_gather_x(value):
    half = value.shape[1] // 2
    a, b = value[:, :half], value[:, half:]
    below_a, above_b = shift_x(a, 1), shift_x(b, -1)
    below_b, above_a = shift_x(b, 1), shift_x(a, -1)
    far_a, far_b = shift_x(below_a, 1), shift_x(above_b, -1)
    return [(a, b), (below_a, below_b), (far_a, far_b), (above_a, above_b)]


def ring_scatter_x(parts, far):
    far_a, far_b = far
    below_b, above_a = shift_x(parts[1][1], 1), shift_x(parts[3][0], -1)
    next_a = (parts[1][0].astype(f32) + far_a.astype(f32)).astype(bf16)
    next_b = (parts[3][1].astype(f32) + far_b.astype(f32)).astype(bf16)
    below_a, above_b = shift_x(next_a, 1), shift_x(next_b, -1)
    return [(below_a, below_b), (above_a, above_b)]


def near_z(value):
    return jnp.stack([shift_z(value, 1), value, shift_z(value, -1)])


def far_z(near):
    low, high = shift_z(near, 3), shift_z(near[:2], -3)
    return [low, near, high]


def side_by_side(pieces, own):
    held = jnp.concatenate(pieces)
    return jnp.concatenate(
        [
            lax.dynamic_index_in_dim(held, (j - own + 4) % NZ, 0, keepdims=False)
            for j in range(NZ)
        ],
        axis=1,
    )


def dot_nt(a, b):
    return lax.dot_general(a, b, (((1,), (1,)), ((), ())), preferred_element_type=f32)


def dot_tn(a, b):
    return lax.dot_general(a, b, (((0,), (0,)), ((), ())), preferred_element_type=f32)


def forward_kernel(
    x_ref, tok_ref, gate_ref, up_ref, down_ref, coef_ref, silu_ref, hid_ref, *rest
):
    outs, (acc_gate, acc_up, made) = rest[: 2 * NX], rest[2 * NX :]
    step = pl.program_id(0)
    width = gate_ref.shape[-1]

    @pl.when(step == 0)
    def _():
        acc_gate[...] = jnp.zeros_like(acc_gate)
        acc_up[...] = jnp.zeros_like(acc_up)

    @pl.when(step < NZ)
    def _():
        block = tok_ref[...]
        gate = gate_ref[...].reshape(-1, width)
        up = up_ref[...].reshape(-1, width)
        acc_gate[...] += jnp.dot(block, gate, preferred_element_type=f32)
        acc_up[...] += jnp.dot(block, up, preferred_element_type=f32)

    @pl.when(step == NZ - 1)
    def _():
        act_gate, act_up = acc_gate[...], acc_up[...]
        sig = jax.nn.sigmoid(act_gate)
        silu_gate = act_gate * sig
        silu_ref[...] = silu_gate
        coef_ref[...] = act_up * (sig * (1.0 + act_gate * (1.0 - sig)))
        hid_ref[...] = (silu_gate * act_up).astype(bf16)

    @pl.when(step >= NZ)
    def _():
        made[...] = jnp.dot(hid_ref[...], down_ref[...], preferred_element_type=f32).astype(bf16)

    for d in range(NX):

        @pl.when(step == NZ + d)
        def _(d=d):
            half = made.shape[1] // 2
            outs[2 * d][...] = made[:, :half]
            outs[2 * d + 1][...] = made[:, half:]


def early_kernel(x_ref, *refs):
    ups, (down_ref, sum_ref, piece) = refs[: 2 * NX - 2], refs[2 * NX - 2 :]
    step = pl.program_id(0)

    for d in range(NX - 1):

        @pl.when(step == d)
        def _(d=d):
            half = piece.shape[1] // 2
            piece[:, :half] = ups[2 * d][...]
            piece[:, half:] = ups[2 * d + 1][...]

    @pl.when(step == 0)
    def _():
        sum_ref[...] = jnp.zeros_like(sum_ref)

    sum_ref[...] += dot_nt(piece[...], down_ref[...])


def backward_kernel(x_ref, *refs):
    far_a, far_b, down_ref, sum_ref, gate_ref, up_ref, coef_ref, silu_ref, hid_ref = refs[:9]
    part_ref, gate_out, up_out, mix = refs[9:]
    step = pl.program_id(0)
    width = gate_ref.shape[-1]
    rows = sum_ref.shape[0]

    @pl.when(step == 0)
    def _():
        half = down_ref.shape[1] // 2
        grad_hidden = sum_ref[...] + dot_nt(far_a[...], down_ref[:, :half])
        grad_hidden += dot_nt(far_b[...], down_ref[:, half:])
        gate_out[...] = (grad_hidden * coef_ref[...]).astype(bf16)
        up_out[...] = (grad_hidden * silu_ref[...]).astype(bf16)
        terms = grad_hidden * hid_ref[...].astype(f32)
        sums = lax.dot_general(
            jnp.ones((8, width), f32),
            terms,
            (((1,), (1,)), ((), ())),
            precision=highest,
            preferred_element_type=f32,
        )
        high, low = high_low(sums)
        cut = part_ref.shape[2]
        tail = jnp.zeros((1, 2 * cut - rows), bf16)
        mix[...] = jnp.concatenate(
            [
                high[:1, :cut],
                jnp.concatenate([high[:1, cut:], tail], axis=1),
                low[:1, :cut],
                jnp.concatenate([low[:1, cut:], tail], axis=1),
                jnp.zeros((4, cut), bf16),
            ]
        )

    @pl.when(step >= 1)
    def _():
        gate = gate_ref[...].reshape(-1, width)
        up = up_ref[...].reshape(-1, width)
        part_ref[0, :rows] = (dot_nt(gate_out[...], gate) + dot_nt(up_out[...], up)).astype(bf16)
        part_ref[0, rows:] = mix[...]


def weight_kernel(x_ref, *refs):
    tok_ref, gact_ref, uact_ref, hid_ref = refs[:4]
    ups = refs[4 : 4 + 2 * NX]
    gate_out, up_out, down_out, piece = refs[4 + 2 * NX :]
    step = pl.program_id(0)

    @pl.when(step < NZ)
    def _():
        block = tok_ref[...]
        gate_out[...] = dot_tn(block, gact_ref[...]).astype(bf16).reshape(gate_out.shape)
        up_out[...] = dot_tn(block, uact_ref[...]).astype(bf16).reshape(up_out.shape)

    for d in range(NX):

        @pl.when(step == NZ + d)
        def _(d=d):
            half = piece.shape[1] // 2
            piece[:, :half] = ups[2 * d][...]
            piece[:, half:] = ups[2 * d + 1][...]

    @pl.when(step >= NZ)
    def _():
        down_out[...] = dot_tn(hid_ref[...], piece[...]).astype(bf16)


def call(kernel, steps, in_specs, out_specs, out_shape, scratch, flops, moved, args):
    return pl.pallas_call(
        kernel,
        grid_spec=pltpu.PrefetchScalarGridSpec(
            num_scalar_prefetch=1,
            grid=(steps,),
            in_specs=in_specs,
            out_specs=out_specs,
            scratch_shapes=scratch,
        ),
        out_shape=out_shape,
        compiler_params=pltpu.CompilerParams(vmem_limit_bytes=63 * 1024 * 1024),
        cost_estimate=pl.CostEstimate(flops=flops, bytes_accessed=moved, transcendentals=0),
    )(*args)


def slot_tables(route_rows, mix_rows, capacity, experts):
    tok_count, top_count = route_rows.shape
    flat_routes = route_rows.reshape(-1)
    onehot = flat_routes[:, None] == jnp.arange(experts, dtype=jnp.int32)[None, :]
    count = tok_count * top_count
    pairs = jnp.arange(count, dtype=jnp.int32)
    before = (pairs[None, :] < pairs[:, None]).astype(bf16)
    earlier = jnp.dot(before, onehot.astype(bf16), preferred_element_type=f32)
    position = jnp.sum(jnp.where(onehot, earlier, 0.0), axis=1).astype(jnp.int32)
    target = (flat_routes * capacity + position).reshape(tok_count, top_count)
    slot_ids = jnp.arange(experts * capacity, dtype=jnp.int32)
    hits = target.T[None, :, :] == slot_ids[:, None, None]
    matches = hits.astype(f32)
    select = jnp.sum(matches, axis=1)
    weighted = jnp.sum(matches * mix_rows.T[None, :, :], axis=1)
    picks = matches.astype(bf16).reshape(experts * capacity, -1)
    return (select.astype(bf16), weighted, picks)


def per_device(tokens, routes, mix_weights, w_gate, w_up, w_down, upstream):
    experts = lax.axis_size("expert")
    section = lax.axis_index("section")
    my_x, my_z = section // NZ, section % NZ
    tok_count, feat = tokens.shape
    top_count = routes.shape[1]
    capacity = 5 * tok_count * top_count // (4 * experts)
    rows = experts * capacity
    ff = w_gate.shape[2]
    wide_x, wide_z = NX * feat, NZ * feat
    full = NX * wide_z
    where = my_x.reshape(1).astype(jnp.int32)
    gate4 = w_gate.reshape(NX, NZ, feat, ff)
    up4 = w_up.reshape(NX, NZ, feat, ff)
    down = w_down[0]

    up_near = near_z(upstream)
    select_low, weighted, picks = slot_tables(routes, mix_weights, capacity, experts)
    slot_scale = jnp.sum(weighted, axis=1)

    def exchange(value):
        return lax.all_to_all(
            value.reshape(experts, -1, value.shape[-1]), "expert", split_axis=0, concat_axis=0, tiled=True
        ).reshape(-1, value.shape[-1])

    tok_sent = jnp.dot(select_low, tokens, preferred_element_type=f32).astype(bf16)
    tok_sent, up_near = lax.optimization_barrier((tok_sent, up_near))
    up_pieces = far_z(up_near)
    tok_rows, up_pieces = lax.optimization_barrier((exchange(tok_sent), up_pieces))
    tok_x = in_order([tok_rows] + [shift_x(tok_rows, d) for d in range(1, NX)], my_x, NX)
    up_z = side_by_side(up_pieces, my_z)
    up_rows = jnp.dot(select_low, up_z, preferred_element_type=f32) * slot_scale[:, None]
    up_rows = exchange(up_rows.astype(bf16))

    dispatched = lax.all_gather(
        tok_x, "section", axis_index_groups=Z_GROUPS, axis=1, tiled=True
    )
    ups = [half for pair in ring_gather_x(up_rows) for half in pair]

    def whole(*shape):
        return pl.BlockSpec(shape, lambda i, s: (0,) * len(shape))

    def clip(i, low, count):
        return jnp.clip(i - low, 0, count - 1)

    def weight_spec(low):
        return pl.BlockSpec((NX, 1, feat, ff), lambda i, s: (0, clip(i, low, NZ), 0, 0))

    def struct(shape, kind):
        return jax.ShapeDtypeStruct(shape, kind)

    tok_spec = pl.BlockSpec((rows, wide_x), lambda i, s: (0, clip(i, 0, NZ)))
    (early,) = call(
        early_kernel,
        NX - 1,
        [whole(rows, wide_z // 2)] * (2 * NX - 2)
        + [
            pl.BlockSpec(
                (ff, wide_z), lambda i, s: (0, (s[0] + jnp.where(i == 1, NX - 1, i // 2)) % NX)
            )
        ],
        [whole(rows, ff)],
        [struct((rows, ff), f32)],
        [pltpu.VMEM((rows, wide_z), bf16)],
        0,
        0,
        (where, *ups[:4], *ups[6:], down),
    )
    dispatched, early = lax.optimization_barrier((dispatched, early))
    coef, silu_gate, hidden, *outs = call(
        forward_kernel,
        NZ + NX,
        [
            tok_spec,
            weight_spec(0),
            weight_spec(0),
            pl.BlockSpec((ff, wide_z), lambda i, s: (0, (s[0] + clip(i, NZ, NX)) % NX)),
        ],
        [whole(rows, ff)] * 3 + [whole(rows, wide_z // 2)] * (2 * NX),
        [struct((rows, ff), f32)] * 2
        + [struct((rows, ff), bf16)]
        + [struct((rows, wide_z // 2), bf16)] * (2 * NX),
        [pltpu.VMEM((rows, ff), f32)] * 2 + [pltpu.VMEM((rows, wide_z), bf16)],
        6 * rows * full * ff,
        2 * (2 * rows * full + 3 * full * ff),
        (where, dispatched, gate4, up4, down),
    )

    outs = [(outs[2 * d], outs[2 * d + 1]) for d in range(NX)]
    far = shift_x(outs[2][0], 1), shift_x(outs[2][1], -1)

    back, gate_act, up_act = call(
        backward_kernel,
        1 + NZ,
        [whole(rows, wide_z // 2)] * 2
        + [pl.BlockSpec((ff, wide_z), lambda i, s: (0, (s[0] + 2) % NX))]
        + [whole(rows, ff)]
        + [weight_spec(1)] * 2
        + [whole(rows, ff)] * 3,
        [pl.BlockSpec((1, rows + 8, wide_x), lambda i, s: (clip(i, 1, NZ), 0, 0))]
        + [whole(rows, ff)] * 2,
        [struct((NZ, rows + 8, wide_x), bf16)] + [struct((rows, ff), bf16)] * 2,
        [pltpu.VMEM((8, wide_x), bf16)],
        0,
        0,
        (where, *ups[4:6], down, early, gate4, up4, coef, silu_gate, hidden),
    )

    back, far = lax.optimization_barrier((back, far))
    sent_x = ring_scatter_x(outs, far)

    back_z = lax.psum_scatter(
        back.reshape(NZ * (rows + 8), wide_x),
        "section",
        axis_index_groups=Z_GROUPS,
        scatter_dimension=0,
        tiled=True,
    )
    grad_gate, grad_up, grad_down = call(
        weight_kernel,
        NZ + NX,
        [tok_spec] + [whole(rows, ff)] * 3 + [whole(rows, wide_z // 2)] * (2 * NX),
        [weight_spec(0)] * 2
        + [pl.BlockSpec((ff, wide_z), lambda i, s: (0, (s[0] + NX - clip(i, NZ, NX)) % NX))],
        [struct((NX, NZ, feat, ff), bf16)] * 2 + [struct((ff, full), bf16)],
        [pltpu.VMEM((rows, wide_z), bf16)],
        0,
        0,
        (where, dispatched, gate_act, up_act, hidden, *ups),
    )

    sent_x, grads = lax.optimization_barrier((sent_x, (grad_gate, grad_up, grad_down)))
    grad_gate, grad_up, grad_down = grads

    summed = jnp.concatenate(
        [
            (outs[0][h].astype(f32) + sent_x[0][h].astype(f32) + sent_x[1][h].astype(f32)).astype(bf16)
            for h in range(2)
        ],
        axis=1,
    )
    returned = exchange(summed)
    moe_out = jnp.dot(weighted.T, returned.astype(f32), precision=highest)
    moe_out, back_z = lax.optimization_barrier((moe_out, back_z))

    mix = back_z[rows : rows + 4].reshape(2, 2 * wide_x)[:, :rows].reshape(2, experts, capacity)
    mix = jnp.pad(mix.transpose(1, 0, 2), ((0, 0), (0, 6), (0, wide_x - capacity)))
    back = exchange(
        jnp.concatenate([back_z[:rows].reshape(experts, capacity, wide_x), mix], axis=1)
    ).reshape(experts, capacity + 8, wide_x)
    mixed = (tokens.astype(f32) + spread_z(moe_out, my_z)).astype(bf16)
    grad_moe = dot_tn(select_low, back[:, :capacity].reshape(rows, wide_x))
    mix = back[:, capacity : capacity + 2, :capacity].transpose(1, 0, 2).reshape(2, rows)
    mix = jnp.sum(jnp.dot(mix, picks, preferred_element_type=f32), axis=0).reshape(-1, feat)
    grad_moe, mix = spread_x(grad_moe, jnp.concatenate(high_low(mix)), my_x)
    grad_tokens = (upstream.astype(f32) + grad_moe).astype(bf16)
    mix = jnp.sum(mix.reshape(2, top_count, tok_count), axis=0)
    grad_mix = mix.T / mix_weights
    return (
        mixed,
        grad_tokens,
        grad_mix,
        grad_gate.reshape(1, full, ff),
        grad_up.reshape(1, full, ff),
        grad_down[None],
    )


def solution(mesh):
    return jax.shard_map(
        per_device,
        mesh=mesh,
        in_specs=(
            P("expert", "section"),
            P("expert", None),
            P("expert", None),
            P("expert", None, "section"),
            P("expert", None, "section"),
            P("expert", "section", None),
            P("expert", "section"),
        ),
        out_specs=(
            P("expert", "section"),
            P("expert", "section"),
            P("expert", None),
            P("expert", None, "section"),
            P("expert", None, "section"),
            P("expert", "section", None),
        ),
        check_vma=False,
    )
```

```python
import functools

import jax
import jax.numpy as jnp
from jax import lax
from jax.experimental import pallas as pl
from jax.experimental.pallas import tpu as pltpu
from jax.sharding import PartitionSpec as P

highest = lax.Precision.HIGHEST
f32, bf16 = jnp.float32, jnp.bfloat16
NX, NZ = 4, 8
PAIR = 2
Z_GROUPS = [[x * NZ + z for z in range(NZ)] for x in range(NX)]


def shift_z(value, d):
    pairs = [(x * NZ + z, x * NZ + (z + d) % NZ) for x in range(NX) for z in range(NZ)]
    return lax.ppermute(value, "section", pairs)


def shift_x(value, d):
    pairs = [(x * NZ + z, ((x + d) % NX) * NZ + z) for x in range(NX) for z in range(NZ)]
    return lax.ppermute(value, "section", pairs)


def in_order(relative, own, count):
    held = jnp.stack(relative)
    return jnp.concatenate(
        [lax.dynamic_index_in_dim(held, (own - j) % count, 0, keepdims=False) for j in range(count)],
        axis=1,
    )


def spread_x(value, extra, own):
    parts = value.reshape(value.shape[0], NX, -1).transpose(1, 0, 2)

    def part(d):
        return lax.dynamic_index_in_dim(parts, (own + d) % NX, 0, keepdims=False)

    sent = [
        shift_x(jnp.concatenate([part(d).astype(bf16), extra]), d).astype(f32) for d in range(1, NX)
    ]
    total = sum(sent, jnp.concatenate([part(0), extra.astype(f32)]))
    return total[: value.shape[0]], total[value.shape[0] :]


def high_low(value):
    high = value.astype(bf16)
    return high, (value - high.astype(f32)).astype(bf16)


def spread_z_far(value, own):
    parts = value.reshape(value.shape[0], NZ, -1).transpose(1, 0, 2)

    def part(d):
        return lax.dynamic_index_in_dim(parts, (own + d) % NZ, 0, keepdims=False)

    above = shift_z(jnp.stack([part(2), part(3), part(4)]).astype(bf16), 3)
    below = shift_z(jnp.stack([part(-3), part(-2)]).astype(bf16), -3)
    return part(-1), part(0), part(1), above, below


def spread_z_near(behind, here, ahead, above, below):
    above, below = above.astype(f32), below.astype(f32)
    right = shift_z((ahead + above[2] + below[1]).astype(bf16), 1)
    left = shift_z((behind + above[0]).astype(bf16), -1)
    return here + above[1] + below[0] + right.astype(f32) + left.astype(f32)


def ring_gather_x(value):
    half = value.shape[1] // 2
    a, b = value[:, :half], value[:, half:]
    below_a, above_b = shift_x(a, 1), shift_x(b, -1)
    below_b, above_a = shift_x(b, 1), shift_x(a, -1)
    far_a, far_b = shift_x(below_a, 1), shift_x(above_b, -1)
    return [(a, b), (below_a, below_b), (far_a, far_b), (above_a, above_b)]


def ring_scatter_x(parts, far):
    far_a, far_b = far
    below_b, above_a = shift_x(parts[1][1], 1), shift_x(parts[3][0], -1)
    next_a = (parts[1][0].astype(f32) + far_a.astype(f32)).astype(bf16)
    next_b = (parts[3][1].astype(f32) + far_b.astype(f32)).astype(bf16)
    below_a, above_b = shift_x(next_a, 1), shift_x(next_b, -1)
    return [(below_a, below_b), (above_a, above_b)]


def near_z(value):
    return jnp.stack([shift_z(value, 1), value, shift_z(value, -1)])


def far_z(near):
    low, high = shift_z(near, 3), shift_z(near[:2], -3)
    return [low, near, high]


def side_by_side(pieces, own):
    held = jnp.concatenate(pieces)
    return jnp.concatenate(
        [
            lax.dynamic_index_in_dim(held, (j - own + 4) % NZ, 0, keepdims=False)
            for j in range(NZ)
        ],
        axis=1,
    )


def dot_nt(a, b):
    return lax.dot_general(a, b, (((1,), (1,)), ((), ())), preferred_element_type=f32)


def dot_tn(a, b):
    return lax.dot_general(a, b, (((0,), (0,)), ((), ())), preferred_element_type=f32)


def weights_by_z(w_ref, gate_ref, up_ref):
    ff = gate_ref.shape[-1]
    for j in range(PAIR):
        block = slice(j * w_ref.shape[0] // PAIR, (j + 1) * w_ref.shape[0] // PAIR)
        w_ref[block, :ff] = gate_ref[:, j].reshape(-1, ff)
        w_ref[block, ff:] = up_ref[:, j].reshape(-1, ff)


def forward_kernel(
    x_ref, tok_ref, gate_ref, up_ref, coef_ref, silu_ref, hid_ref, acc, weights
):
    step = pl.program_id(0)
    ff = gate_ref.shape[-1]

    @pl.when(step == 0)
    def _():
        acc[...] = jnp.zeros_like(acc)

    weights_by_z(weights, gate_ref, up_ref)
    acc[...] += jnp.dot(tok_ref[...], weights[...], preferred_element_type=f32)

    @pl.when(step == NZ // PAIR - 1)
    def _():
        act_gate, act_up = acc[:, :ff], acc[:, ff:]
        sig = jax.nn.sigmoid(act_gate)
        silu_gate = act_gate * sig
        silu_ref[...] = silu_gate
        coef_ref[...] = act_up * (sig * (1.0 + act_gate * (1.0 - sig)))
        hid_ref[...] = (silu_gate * act_up).astype(bf16)


def output_kernel(x_ref, hid_ref, down_ref, *rest):
    outs, made = rest[: 2 * NX], rest[2 * NX]
    step = pl.program_id(0)
    made[...] = jnp.dot(hid_ref[...], down_ref[...], preferred_element_type=f32).astype(bf16)

    for d in range(NX):

        @pl.when(step == d)
        def _(d=d):
            half = made.shape[1] // 2
            outs[2 * d][...] = made[:, :half]
            outs[2 * d + 1][...] = made[:, half:]


def early_kernel(x_ref, *refs):
    ups, (down_ref, sum_ref, piece) = refs[: 2 * NX - 2], refs[2 * NX - 2 :]
    step = pl.program_id(0)

    for d in range(NX - 1):

        @pl.when(step == d)
        def _(d=d):
            half = piece.shape[1] // 2
            piece[:, :half] = ups[2 * d][...]
            piece[:, half:] = ups[2 * d + 1][...]

    @pl.when(step == 0)
    def _():
        sum_ref[...] = jnp.zeros_like(sum_ref)

    sum_ref[...] += dot_nt(piece[...], down_ref[...])


def backward_kernel(x_ref, *refs):
    far_a, far_b, down_ref, sum_ref, gate_ref, up_ref, coef_ref, silu_ref, hid_ref = refs[:9]
    part_ref, act_out, mix, weights = refs[9:]
    step = pl.program_id(0)
    width = gate_ref.shape[-1]
    rows = sum_ref.shape[0]

    @pl.when(step == 0)
    def _():
        half = down_ref.shape[1] // 2
        grad_hidden = sum_ref[...] + dot_nt(far_a[...], down_ref[:, :half])
        grad_hidden += dot_nt(far_b[...], down_ref[:, half:])
        act_out[:, :width] = (grad_hidden * coef_ref[...]).astype(bf16)
        act_out[:, width:] = (grad_hidden * silu_ref[...]).astype(bf16)
        terms = grad_hidden * hid_ref[...].astype(f32)
        sums = lax.dot_general(
            jnp.ones((8, width), f32),
            terms,
            (((1,), (1,)), ((), ())),
            precision=highest,
            preferred_element_type=f32,
        )
        high, low = high_low(sums)
        cut = part_ref.shape[2]
        tail = jnp.zeros((1, 2 * cut - rows), bf16)
        mix[...] = jnp.concatenate(
            [
                high[:1, :cut],
                jnp.concatenate([high[:1, cut:], tail], axis=1),
                low[:1, :cut],
                jnp.concatenate([low[:1, cut:], tail], axis=1),
                jnp.zeros((4, cut), bf16),
            ]
        )

    @pl.when(step >= 1)
    def _():
        weights_by_z(weights, gate_ref, up_ref)
        part = dot_nt(act_out[...], weights[...]).astype(bf16)
        cut = part_ref.shape[2]
        for j in range(PAIR):
            part_ref[j, :rows] = part[:, j * cut : (j + 1) * cut]
            part_ref[j, rows:] = mix[...]


def weight_kernel(x_ref, *refs):
    tok_ref, act_ref, hid_ref = refs[:3]
    ups = refs[3 : 3 + 2 * NX]
    gate_out, up_out, down_out, piece = refs[3 + 2 * NX :]
    step = pl.program_id(0)
    first = NZ // PAIR
    ff = hid_ref.shape[1]

    @pl.when(step < first)
    def _():
        grad = dot_tn(tok_ref[...], act_ref[...]).astype(bf16)
        for j in range(PAIR):
            block = grad[j * grad.shape[0] // PAIR : (j + 1) * grad.shape[0] // PAIR]
            gate_out[:, j] = block[:, :ff].reshape(NX, -1, ff)
            up_out[:, j] = block[:, ff:].reshape(NX, -1, ff)

    for d in range(NX):

        @pl.when(step == first + d)
        def _(d=d):
            half = piece.shape[1] // 2
            piece[:, :half] = ups[2 * d][...]
            piece[:, half:] = ups[2 * d + 1][...]

    @pl.when(step >= first)
    def _():
        down_out[...] = dot_tn(hid_ref[...], piece[...]).astype(bf16)


def call(kernel, steps, in_specs, out_specs, out_shape, scratch, flops, moved, args):
    return pl.pallas_call(
        kernel,
        grid_spec=pltpu.PrefetchScalarGridSpec(
            num_scalar_prefetch=1,
            grid=(steps,),
            in_specs=in_specs,
            out_specs=out_specs,
            scratch_shapes=scratch,
        ),
        out_shape=out_shape,
        compiler_params=pltpu.CompilerParams(vmem_limit_bytes=63 * 1024 * 1024),
        cost_estimate=pl.CostEstimate(flops=flops, bytes_accessed=moved, transcendentals=0),
    )(*args)


def slot_tables(route_rows, mix_rows, capacity, experts):
    tok_count, top_count = route_rows.shape
    flat_routes = route_rows.reshape(-1)
    onehot = flat_routes[:, None] == jnp.arange(experts, dtype=jnp.int32)[None, :]
    count = tok_count * top_count
    pairs = jnp.arange(count, dtype=jnp.int32)
    before = (pairs[None, :] < pairs[:, None]).astype(bf16)
    earlier = jnp.dot(before, onehot.astype(bf16), preferred_element_type=f32)
    position = jnp.sum(jnp.where(onehot, earlier, 0.0), axis=1).astype(jnp.int32)
    target = (flat_routes * capacity + position).reshape(tok_count, top_count)
    slot_ids = jnp.arange(experts * capacity, dtype=jnp.int32)
    hits = target.T[None, :, :] == slot_ids[:, None, None]
    matches = hits.astype(f32)
    select = jnp.sum(matches, axis=1)
    weighted = jnp.sum(matches * mix_rows.T[None, :, :], axis=1)
    picks = matches.astype(bf16).reshape(experts * capacity, -1)
    return (select.astype(bf16), weighted, picks)


def per_device(tokens, routes, mix_weights, w_gate, w_up, w_down, upstream):
    experts = lax.axis_size("expert")
    section = lax.axis_index("section")
    my_x, my_z = section // NZ, section % NZ
    tok_count, feat = tokens.shape
    top_count = routes.shape[1]
    capacity = 5 * tok_count * top_count // (4 * experts)
    rows = experts * capacity
    ff = w_gate.shape[2]
    wide_x, wide_z = NX * feat, NZ * feat
    full = NX * wide_z
    where = my_x.reshape(1).astype(jnp.int32)
    gate4 = w_gate.reshape(NX, NZ, feat, ff)
    up4 = w_up.reshape(NX, NZ, feat, ff)
    down = w_down[0]

    up_near = near_z(upstream)
    select_low, weighted, picks = slot_tables(routes, mix_weights, capacity, experts)
    slot_scale = jnp.sum(weighted, axis=1)

    def exchange(value):
        return lax.all_to_all(
            value.reshape(experts, -1, value.shape[-1]), "expert", split_axis=0, concat_axis=0, tiled=True
        ).reshape(-1, value.shape[-1])

    tok_sent = jnp.dot(select_low, tokens, preferred_element_type=f32).astype(bf16)
    tok_sent, up_near = lax.optimization_barrier((tok_sent, up_near))
    up_pieces = far_z(up_near)
    tok_rows, up_pieces = lax.optimization_barrier((exchange(tok_sent), up_pieces))
    tok_x = in_order([tok_rows] + [shift_x(tok_rows, d) for d in range(1, NX)], my_x, NX)
    up_z = side_by_side(up_pieces, my_z)
    up_rows = jnp.dot(select_low, up_z, preferred_element_type=f32) * slot_scale[:, None]
    up_rows = exchange(up_rows.astype(bf16))

    dispatched = lax.all_gather(
        tok_x, "section", axis_index_groups=Z_GROUPS, axis=1, tiled=True
    )
    ups = [half for pair in ring_gather_x(up_rows) for half in pair]

    def whole(*shape):
        return pl.BlockSpec(shape, lambda i, s: (0,) * len(shape))

    def clip(i, low, count):
        return jnp.clip(i - low, 0, count - 1)

    def weight_spec(low):
        return pl.BlockSpec(
            (NX, PAIR, feat, ff), lambda i, s: (0, clip(i, low, NZ // PAIR), 0, 0)
        )

    def struct(shape, kind):
        return jax.ShapeDtypeStruct(shape, kind)

    tok_spec = pl.BlockSpec((rows, PAIR * wide_x), lambda i, s: (0, clip(i, 0, NZ // PAIR)))
    weight_scratch = pltpu.VMEM((PAIR * wide_x, 2 * ff), bf16)
    (early,) = call(
        early_kernel,
        NX - 1,
        [whole(rows, wide_z // 2)] * (2 * NX - 2)
        + [
            pl.BlockSpec(
                (ff, wide_z), lambda i, s: (0, (s[0] + jnp.where(i == 1, NX - 1, i // 2)) % NX)
            )
        ],
        [whole(rows, ff)],
        [struct((rows, ff), f32)],
        [pltpu.VMEM((rows, wide_z), bf16)],
        0,
        0,
        (where, *ups[:4], *ups[6:], down),
    )
    dispatched, early = lax.optimization_barrier((dispatched, early))
    coef, silu_gate, hidden = call(
        forward_kernel,
        NZ // PAIR,
        [tok_spec, weight_spec(0), weight_spec(0)],
        [whole(rows, ff)] * 3,
        [struct((rows, ff), f32)] * 2 + [struct((rows, ff), bf16)],
        [pltpu.VMEM((rows, 2 * ff), f32), weight_scratch],
        4 * rows * full * ff,
        2 * (rows * full + 2 * full * ff),
        (where, dispatched, gate4, up4),
    )

    back, grad_act = call(
        backward_kernel,
        1 + NZ // PAIR,
        [whole(rows, wide_z // 2)] * 2
        + [pl.BlockSpec((ff, wide_z), lambda i, s: (0, (s[0] + 2) % NX))]
        + [whole(rows, ff)]
        + [weight_spec(1)] * 2
        + [whole(rows, ff)] * 3,
        [
            pl.BlockSpec(
                (PAIR, rows + 8, wide_x), lambda i, s: (clip(i, 1, NZ // PAIR), 0, 0)
            ),
            whole(rows, 2 * ff),
        ],
        [struct((NZ, rows + 8, wide_x), bf16), struct((rows, 2 * ff), bf16)],
        [pltpu.VMEM((8, wide_x), bf16), weight_scratch],
        0,
        0,
        (where, *ups[4:6], down, early, gate4, up4, coef, silu_gate, hidden),
    )

    hidden, grad_act = lax.optimization_barrier((hidden, grad_act))
    outs = call(
        output_kernel,
        NX,
        [whole(rows, ff), pl.BlockSpec((ff, wide_z), lambda i, s: (0, (s[0] + i) % NX))],
        [whole(rows, wide_z // 2)] * (2 * NX),
        [struct((rows, wide_z // 2), bf16)] * (2 * NX),
        [pltpu.VMEM((rows, wide_z), bf16)],
        0,
        0,
        (where, hidden, down),
    )
    outs = [(outs[2 * d], outs[2 * d + 1]) for d in range(NX)]
    far = shift_x(outs[2][0], 1), shift_x(outs[2][1], -1)
    sent_x = ring_scatter_x(outs, far)

    back_z = lax.psum_scatter(
        back.reshape(NZ * (rows + 8), wide_x),
        "section",
        axis_index_groups=Z_GROUPS,
        scatter_dimension=0,
        tiled=True,
    )
    grad_gate, grad_up, grad_down = call(
        weight_kernel,
        NZ // PAIR + NX,
        [tok_spec, whole(rows, 2 * ff), whole(rows, ff)]
        + [whole(rows, wide_z // 2)] * (2 * NX),
        [weight_spec(0)] * 2
        + [pl.BlockSpec((ff, wide_z), lambda i, s: (0, (s[0] + NX - clip(i, NZ // PAIR, NX)) % NX))],
        [struct((NX, NZ, feat, ff), bf16)] * 2 + [struct((ff, full), bf16)],
        [pltpu.VMEM((rows, wide_z), bf16)],
        0,
        0,
        (where, dispatched, grad_act, hidden, *ups),
    )

    sent_x, grads = lax.optimization_barrier((sent_x, (grad_gate, grad_up, grad_down)))
    grad_gate, grad_up, grad_down = grads

    summed = jnp.concatenate(
        [
            (outs[0][h].astype(f32) + sent_x[0][h].astype(f32) + sent_x[1][h].astype(f32)).astype(bf16)
            for h in range(2)
        ],
        axis=1,
    )
    returned = exchange(summed)
    moe_out = jnp.dot(weighted.T, returned.astype(f32), precision=highest)

    mix = back_z[rows : rows + 4].reshape(2, 2 * wide_x)[:, :rows].reshape(2, experts, capacity)
    mix = jnp.pad(mix.transpose(1, 0, 2), ((0, 0), (0, 6), (0, wide_x - capacity)))
    back = exchange(
        jnp.concatenate([back_z[:rows].reshape(experts, capacity, wide_x), mix], axis=1)
    ).reshape(experts, capacity + 8, wide_x)
    moe_parts, back = lax.optimization_barrier((spread_z_far(moe_out, my_z), back))
    mixed = (tokens.astype(f32) + spread_z_near(*moe_parts)).astype(bf16)
    grad_moe = dot_tn(select_low, back[:, :capacity].reshape(rows, wide_x))
    mix = back[:, capacity : capacity + 2, :capacity].transpose(1, 0, 2).reshape(2, rows)
    mix = jnp.sum(jnp.dot(mix, picks, preferred_element_type=f32), axis=0).reshape(-1, feat)
    grad_moe, mix = spread_x(grad_moe, jnp.concatenate(high_low(mix)), my_x)
    grad_tokens = (upstream.astype(f32) + grad_moe).astype(bf16)
    mix = jnp.sum(mix.reshape(2, top_count, tok_count), axis=0)
    grad_mix = mix.T / mix_weights
    return (
        mixed,
        grad_tokens,
        grad_mix,
        grad_gate.reshape(1, full, ff),
        grad_up.reshape(1, full, ff),
        grad_down[None],
    )


def solution(mesh):
    return jax.shard_map(
        per_device,
        mesh=mesh,
        in_specs=(
            P("expert", "section"),
            P("expert", None),
            P("expert", None),
            P("expert", None, "section"),
            P("expert", None, "section"),
            P("expert", "section", None),
            P("expert", "section"),
        ),
        out_specs=(
            P("expert", "section"),
            P("expert", "section"),
            P("expert", None),
            P("expert", None, "section"),
            P("expert", None, "section"),
            P("expert", "section", None),
        ),
        check_vma=False,
    )
```

```python
import functools

import jax
import jax.numpy as jnp
from jax import lax
from jax.experimental import pallas as pl
from jax.experimental.pallas import tpu as pltpu
from jax.sharding import PartitionSpec as P

highest = lax.Precision.HIGHEST
f32, bf16 = jnp.float32, jnp.bfloat16
NX, NZ = 4, 8
PAIR = 2
Z_GROUPS = [[x * NZ + z for z in range(NZ)] for x in range(NX)]


def shift_z(value, d):
    pairs = [(x * NZ + z, x * NZ + (z + d) % NZ) for x in range(NX) for z in range(NZ)]
    return lax.ppermute(value, "section", pairs)


def shift_x(value, d):
    pairs = [(x * NZ + z, ((x + d) % NX) * NZ + z) for x in range(NX) for z in range(NZ)]
    return lax.ppermute(value, "section", pairs)


def in_order(relative, own, count):
    held = jnp.stack(relative)
    return jnp.concatenate(
        [lax.dynamic_index_in_dim(held, (own - j) % count, 0, keepdims=False) for j in range(count)],
        axis=1,
    )


def spread_x(value, extra, own):
    parts = value.reshape(value.shape[0], NX, -1).transpose(1, 0, 2)

    def part(d):
        return lax.dynamic_index_in_dim(parts, (own + d) % NX, 0, keepdims=False)

    sent = [
        shift_x(jnp.concatenate([part(d).astype(bf16), extra]), d).astype(f32) for d in range(1, NX)
    ]
    total = sum(sent, jnp.concatenate([part(0), extra.astype(f32)]))
    return total[: value.shape[0]], total[value.shape[0] :]


def high_low(value):
    high = value.astype(bf16)
    return high, (value - high.astype(f32)).astype(bf16)


def spread_z_far(value, own):
    parts = value.reshape(value.shape[0], NZ, -1).transpose(1, 0, 2)

    def part(d):
        return lax.dynamic_index_in_dim(parts, (own + d) % NZ, 0, keepdims=False)

    above = shift_z(jnp.stack([part(2), part(3), part(4)]).astype(bf16), 3)
    below = shift_z(jnp.stack([part(-3), part(-2)]).astype(bf16), -3)
    return part(-1), part(0), part(1), above, below


def spread_z_near(behind, here, ahead, above, below):
    above, below = above.astype(f32), below.astype(f32)
    right = shift_z((ahead + above[2] + below[1]).astype(bf16), 1)
    left = shift_z((behind + above[0]).astype(bf16), -1)
    return here + above[1] + below[0] + right.astype(f32) + left.astype(f32)


def ring_gather_x(value):
    half = value.shape[1] // 2
    a, b = value[:, :half], value[:, half:]
    below_a, above_b = shift_x(a, 1), shift_x(b, -1)
    below_b, above_a = shift_x(b, 1), shift_x(a, -1)
    far_a, far_b = shift_x(below_a, 1), shift_x(above_b, -1)
    return [(a, b), (below_a, below_b), (far_a, far_b), (above_a, above_b)]


def ring_scatter_x(parts, far):
    far_a, far_b = far
    below_b, above_a = shift_x(parts[1][1], 1), shift_x(parts[3][0], -1)
    next_a = (parts[1][0].astype(f32) + far_a.astype(f32)).astype(bf16)
    next_b = (parts[3][1].astype(f32) + far_b.astype(f32)).astype(bf16)
    below_a, above_b = shift_x(next_a, 1), shift_x(next_b, -1)
    return [(below_a, below_b), (above_a, above_b)]


def near_z(value):
    return jnp.stack([shift_z(value, 1), value, shift_z(value, -1)])


def far_z(near):
    low, high = shift_z(near, 3), shift_z(near[:2], -3)
    return [low, near, high]


def side_by_side(pieces, own):
    held = jnp.concatenate(pieces)
    return jnp.concatenate(
        [
            lax.dynamic_index_in_dim(held, (j - own + 4) % NZ, 0, keepdims=False)
            for j in range(NZ)
        ],
        axis=1,
    )


def dot_nt(a, b):
    return lax.dot_general(a, b, (((1,), (1,)), ((), ())), preferred_element_type=f32)


def dot_tn(a, b):
    return lax.dot_general(a, b, (((0,), (0,)), ((), ())), preferred_element_type=f32)


def weights_by_z(w_ref, gate_ref, up_ref):
    ff = gate_ref.shape[-1]
    for j in range(PAIR):
        block = slice(j * w_ref.shape[0] // PAIR, (j + 1) * w_ref.shape[0] // PAIR)
        w_ref[block, :ff] = gate_ref[:, j].reshape(-1, ff)
        w_ref[block, ff:] = up_ref[:, j].reshape(-1, ff)


def forward_kernel(
    x_ref, tok_ref, gate_ref, up_ref, coef_ref, silu_ref, hid_ref, acc, weights
):
    step = pl.program_id(0)
    ff = gate_ref.shape[-1]

    @pl.when(step == 0)
    def _():
        acc[...] = jnp.zeros_like(acc)

    weights_by_z(weights, gate_ref, up_ref)
    acc[...] += jnp.dot(tok_ref[...], weights[...], preferred_element_type=f32)

    @pl.when(step == NZ // PAIR - 1)
    def _():
        act_gate, act_up = acc[:, :ff], acc[:, ff:]
        sig = jax.nn.sigmoid(act_gate)
        silu_gate = act_gate * sig
        silu_ref[...] = silu_gate
        coef_ref[...] = act_up * (sig * (1.0 + act_gate * (1.0 - sig)))
        hid_ref[...] = (silu_gate * act_up).astype(bf16)


def output_kernel(x_ref, hid_ref, down_ref, *rest):
    outs, made = rest[:-1], rest[-1]
    step = pl.program_id(0)
    made[...] = jnp.dot(hid_ref[...], down_ref[...], preferred_element_type=f32).astype(bf16)

    for d in range(len(outs) // 2):

        @pl.when(step == d)
        def _(d=d):
            half = made.shape[1] // 2
            outs[2 * d][...] = made[:, :half]
            outs[2 * d + 1][...] = made[:, half:]


def early_kernel(x_ref, *refs):
    ups, (down_ref, sum_ref, piece) = refs[: 2 * NX - 2], refs[2 * NX - 2 :]
    step = pl.program_id(0)

    for d in range(NX - 1):

        @pl.when(step == d)
        def _(d=d):
            half = piece.shape[1] // 2
            piece[:, :half] = ups[2 * d][...]
            piece[:, half:] = ups[2 * d + 1][...]

    @pl.when(step == 0)
    def _():
        sum_ref[...] = jnp.zeros_like(sum_ref)

    sum_ref[...] += dot_nt(piece[...], down_ref[...])


def backward_kernel(x_ref, *refs):
    far_a, far_b, down_ref, sum_ref, gate_ref, up_ref, coef_ref, silu_ref, hid_ref = refs[:9]
    part_ref, act_out, mix, weights = refs[9:]
    step = pl.program_id(0)
    width = gate_ref.shape[-1]
    rows = sum_ref.shape[0]

    @pl.when(step == 0)
    def _():
        half = down_ref.shape[1] // 2
        grad_hidden = sum_ref[...] + dot_nt(far_a[...], down_ref[:, :half])
        grad_hidden += dot_nt(far_b[...], down_ref[:, half:])
        act_out[:, :width] = (grad_hidden * coef_ref[...]).astype(bf16)
        act_out[:, width:] = (grad_hidden * silu_ref[...]).astype(bf16)
        terms = grad_hidden * hid_ref[...].astype(f32)
        sums = lax.dot_general(
            jnp.ones((8, width), f32),
            terms,
            (((1,), (1,)), ((), ())),
            precision=highest,
            preferred_element_type=f32,
        )
        high, low = high_low(sums)
        cut = part_ref.shape[2]
        tail = jnp.zeros((1, 2 * cut - rows), bf16)
        mix[...] = jnp.concatenate(
            [
                high[:1, :cut],
                jnp.concatenate([high[:1, cut:], tail], axis=1),
                low[:1, :cut],
                jnp.concatenate([low[:1, cut:], tail], axis=1),
                jnp.zeros((4, cut), bf16),
            ]
        )

    @pl.when(step >= 1)
    def _():
        weights_by_z(weights, gate_ref, up_ref)
        part = dot_nt(act_out[...], weights[...]).astype(bf16)
        cut = part_ref.shape[2]
        for j in range(PAIR):
            part_ref[j, :rows] = part[:, j * cut : (j + 1) * cut]
            part_ref[j, rows:] = mix[...]


def weight_kernel(x_ref, *refs):
    tok_ref, act_ref, hid_ref = refs[:3]
    ups = refs[3 : 3 + 2 * NX]
    gate_out, up_out, down_out, piece = refs[3 + 2 * NX :]
    step = pl.program_id(0)
    first = NZ // PAIR
    ff = hid_ref.shape[1]

    @pl.when(step < first)
    def _():
        grad = dot_tn(tok_ref[...], act_ref[...]).astype(bf16)
        for j in range(PAIR):
            block = grad[j * grad.shape[0] // PAIR : (j + 1) * grad.shape[0] // PAIR]
            gate_out[:, j] = block[:, :ff].reshape(NX, -1, ff)
            up_out[:, j] = block[:, ff:].reshape(NX, -1, ff)

    for d in range(NX):

        @pl.when(step == first + d)
        def _(d=d):
            half = piece.shape[1] // 2
            piece[:, :half] = ups[2 * d][...]
            piece[:, half:] = ups[2 * d + 1][...]

    @pl.when(step >= first)
    def _():
        down_out[...] = dot_tn(hid_ref[...], piece[...]).astype(bf16)


def call(kernel, steps, in_specs, out_specs, out_shape, scratch, flops, moved, args):
    return pl.pallas_call(
        kernel,
        grid_spec=pltpu.PrefetchScalarGridSpec(
            num_scalar_prefetch=1,
            grid=(steps,),
            in_specs=in_specs,
            out_specs=out_specs,
            scratch_shapes=scratch,
        ),
        out_shape=out_shape,
        compiler_params=pltpu.CompilerParams(vmem_limit_bytes=63 * 1024 * 1024),
        cost_estimate=pl.CostEstimate(flops=flops, bytes_accessed=moved, transcendentals=0),
    )(*args)


def slot_tables(route_rows, mix_rows, capacity, experts):
    tok_count, top_count = route_rows.shape
    flat_routes = route_rows.reshape(-1)
    onehot = flat_routes[:, None] == jnp.arange(experts, dtype=jnp.int32)[None, :]
    count = tok_count * top_count
    pairs = jnp.arange(count, dtype=jnp.int32)
    before = (pairs[None, :] < pairs[:, None]).astype(bf16)
    earlier = jnp.dot(before, onehot.astype(bf16), preferred_element_type=f32)
    position = jnp.sum(jnp.where(onehot, earlier, 0.0), axis=1).astype(jnp.int32)
    target = (flat_routes * capacity + position).reshape(tok_count, top_count)
    slot_ids = jnp.arange(experts * capacity, dtype=jnp.int32)
    hits = target.T[None, :, :] == slot_ids[:, None, None]
    matches = hits.astype(f32)
    select = jnp.sum(matches, axis=1)
    weighted = jnp.sum(matches * mix_rows.T[None, :, :], axis=1)
    picks = matches.astype(bf16).reshape(experts * capacity, -1)
    return (select.astype(bf16), weighted, picks)


def per_device(tokens, routes, mix_weights, w_gate, w_up, w_down, upstream):
    experts = lax.axis_size("expert")
    section = lax.axis_index("section")
    my_x, my_z = section // NZ, section % NZ
    tok_count, feat = tokens.shape
    top_count = routes.shape[1]
    capacity = 5 * tok_count * top_count // (4 * experts)
    rows = experts * capacity
    ff = w_gate.shape[2]
    wide_x, wide_z = NX * feat, NZ * feat
    full = NX * wide_z
    where = my_x.reshape(1).astype(jnp.int32)
    gate4 = w_gate.reshape(NX, NZ, feat, ff)
    up4 = w_up.reshape(NX, NZ, feat, ff)
    down = w_down[0]

    up_near = near_z(upstream)
    select_low, weighted, picks = slot_tables(routes, mix_weights, capacity, experts)
    slot_scale = jnp.sum(weighted, axis=1)

    def exchange(value):
        return lax.all_to_all(
            value.reshape(experts, -1, value.shape[-1]), "expert", split_axis=0, concat_axis=0, tiled=True
        ).reshape(-1, value.shape[-1])

    tok_sent = jnp.dot(select_low, tokens, preferred_element_type=f32).astype(bf16)
    tok_sent, up_near = lax.optimization_barrier((tok_sent, up_near))
    up_pieces = far_z(up_near)
    tok_rows, up_pieces = lax.optimization_barrier((exchange(tok_sent), up_pieces))
    tok_x = in_order([tok_rows] + [shift_x(tok_rows, d) for d in range(1, NX)], my_x, NX)
    up_z = side_by_side(up_pieces, my_z)
    up_rows = jnp.dot(select_low, up_z, preferred_element_type=f32) * slot_scale[:, None]
    up_rows = exchange(up_rows.astype(bf16))

    dispatched = lax.all_gather(
        tok_x, "section", axis_index_groups=Z_GROUPS, axis=1, tiled=True
    )
    ups = [half for pair in ring_gather_x(up_rows) for half in pair]

    def whole(*shape):
        return pl.BlockSpec(shape, lambda i, s: (0,) * len(shape))

    def clip(i, low, count):
        return jnp.clip(i - low, 0, count - 1)

    def weight_spec(low):
        return pl.BlockSpec(
            (NX, PAIR, feat, ff), lambda i, s: (0, clip(i, low, NZ // PAIR), 0, 0)
        )

    def struct(shape, kind):
        return jax.ShapeDtypeStruct(shape, kind)

    tok_spec = pl.BlockSpec((rows, PAIR * wide_x), lambda i, s: (0, clip(i, 0, NZ // PAIR)))
    weight_scratch = pltpu.VMEM((PAIR * wide_x, 2 * ff), bf16)
    (early,) = call(
        early_kernel,
        NX - 1,
        [whole(rows, wide_z // 2)] * (2 * NX - 2)
        + [
            pl.BlockSpec(
                (ff, wide_z), lambda i, s: (0, (s[0] + jnp.where(i == 1, NX - 1, i // 2)) % NX)
            )
        ],
        [whole(rows, ff)],
        [struct((rows, ff), f32)],
        [pltpu.VMEM((rows, wide_z), bf16)],
        0,
        0,
        (where, *ups[:4], *ups[6:], down),
    )
    dispatched, early = lax.optimization_barrier((dispatched, early))
    coef, silu_gate, hidden = call(
        forward_kernel,
        NZ // PAIR,
        [tok_spec, weight_spec(0), weight_spec(0)],
        [whole(rows, ff)] * 3,
        [struct((rows, ff), f32)] * 2 + [struct((rows, ff), bf16)],
        [pltpu.VMEM((rows, 2 * ff), f32), weight_scratch],
        4 * rows * full * ff,
        2 * (rows * full + 2 * full * ff),
        (where, dispatched, gate4, up4),
    )

    def outputs(hidden, steps, place):
        outs = call(
            output_kernel,
            steps,
            [
                whole(rows, ff),
                pl.BlockSpec((ff, wide_z), lambda i, s: (0, (s[0] + place(i)) % NX)),
            ],
            [whole(rows, wide_z // 2)] * (2 * steps),
            [struct((rows, wide_z // 2), bf16)] * (2 * steps),
            [pltpu.VMEM((rows, wide_z), bf16)],
            0,
            0,
            (where, hidden, down),
        )
        return [(outs[2 * d], outs[2 * d + 1]) for d in range(steps)]

    (farthest,) = outputs(hidden, 1, lambda i: 2)
    far = shift_x(farthest[0], 1), shift_x(farthest[1], -1)

    back, grad_act = call(
        backward_kernel,
        1 + NZ // PAIR,
        [whole(rows, wide_z // 2)] * 2
        + [pl.BlockSpec((ff, wide_z), lambda i, s: (0, (s[0] + 2) % NX))]
        + [whole(rows, ff)]
        + [weight_spec(1)] * 2
        + [whole(rows, ff)] * 3,
        [
            pl.BlockSpec(
                (PAIR, rows + 8, wide_x), lambda i, s: (clip(i, 1, NZ // PAIR), 0, 0)
            ),
            whole(rows, 2 * ff),
        ],
        [struct((NZ, rows + 8, wide_x), bf16), struct((rows, 2 * ff), bf16)],
        [pltpu.VMEM((8, wide_x), bf16), weight_scratch],
        0,
        0,
        (where, *ups[4:6], down, early, gate4, up4, coef, silu_gate, hidden),
    )

    hidden, grad_act = lax.optimization_barrier((hidden, grad_act))
    own, above, below = outputs(hidden, 3, lambda i: i + i // 2)
    back, far, own, above, below = lax.optimization_barrier((back, far, own, above, below))
    outs = [own, above, None, below]
    sent_x = ring_scatter_x(outs, far)

    back_z = lax.psum_scatter(
        back.reshape(NZ * (rows + 8), wide_x),
        "section",
        axis_index_groups=Z_GROUPS,
        scatter_dimension=0,
        tiled=True,
    )
    grad_gate, grad_up, grad_down = call(
        weight_kernel,
        NZ // PAIR + NX,
        [tok_spec, whole(rows, 2 * ff), whole(rows, ff)]
        + [whole(rows, wide_z // 2)] * (2 * NX),
        [weight_spec(0)] * 2
        + [pl.BlockSpec((ff, wide_z), lambda i, s: (0, (s[0] + NX - clip(i, NZ // PAIR, NX)) % NX))],
        [struct((NX, NZ, feat, ff), bf16)] * 2 + [struct((ff, full), bf16)],
        [pltpu.VMEM((rows, wide_z), bf16)],
        0,
        0,
        (where, dispatched, grad_act, hidden, *ups),
    )

    sent_x, grads = lax.optimization_barrier((sent_x, (grad_gate, grad_up, grad_down)))
    grad_gate, grad_up, grad_down = grads

    summed = jnp.concatenate(
        [
            (outs[0][h].astype(f32) + sent_x[0][h].astype(f32) + sent_x[1][h].astype(f32)).astype(bf16)
            for h in range(2)
        ],
        axis=1,
    )
    returned = exchange(summed)
    moe_out = jnp.dot(weighted.T, returned.astype(f32), precision=highest)
    moe_out, back_z = lax.optimization_barrier((moe_out, back_z))

    mix = back_z[rows : rows + 4].reshape(2, 2 * wide_x)[:, :rows].reshape(2, experts, capacity)
    mix = jnp.pad(mix.transpose(1, 0, 2), ((0, 0), (0, 6), (0, wide_x - capacity)))
    back = exchange(
        jnp.concatenate([back_z[:rows].reshape(experts, capacity, wide_x), mix], axis=1)
    ).reshape(experts, capacity + 8, wide_x)
    moe_parts, back = lax.optimization_barrier((spread_z_far(moe_out, my_z), back))
    mixed = (tokens.astype(f32) + spread_z_near(*moe_parts)).astype(bf16)
    grad_moe = dot_tn(select_low, back[:, :capacity].reshape(rows, wide_x))
    mix = back[:, capacity : capacity + 2, :capacity].transpose(1, 0, 2).reshape(2, rows)
    mix = jnp.sum(jnp.dot(mix, picks, preferred_element_type=f32), axis=0).reshape(-1, feat)
    grad_moe, mix = spread_x(grad_moe, jnp.concatenate(high_low(mix)), my_x)
    grad_tokens = (upstream.astype(f32) + grad_moe).astype(bf16)
    mix = jnp.sum(mix.reshape(2, top_count, tok_count), axis=0)
    grad_mix = mix.T / mix_weights
    return (
        mixed,
        grad_tokens,
        grad_mix,
        grad_gate.reshape(1, full, ff),
        grad_up.reshape(1, full, ff),
        grad_down[None],
    )


def solution(mesh):
    return jax.shard_map(
        per_device,
        mesh=mesh,
        in_specs=(
            P("expert", "section"),
            P("expert", None),
            P("expert", None),
            P("expert", None, "section"),
            P("expert", None, "section"),
            P("expert", "section", None),
            P("expert", "section"),
        ),
        out_specs=(
            P("expert", "section"),
            P("expert", "section"),
            P("expert", None),
            P("expert", None, "section"),
            P("expert", None, "section"),
            P("expert", "section", None),
        ),
        check_vma=False,
    )
```

```python
import functools

import jax
import jax.numpy as jnp
from jax import lax
from jax.experimental import pallas as pl
from jax.experimental.pallas import tpu as pltpu
from jax.sharding import PartitionSpec as P

highest = lax.Precision.HIGHEST
f32, bf16 = jnp.float32, jnp.bfloat16
NX, NZ = 4, 8
PAIR = 2
Z_GROUPS = [[x * NZ + z for z in range(NZ)] for x in range(NX)]


def shift_z(value, d):
    pairs = [(x * NZ + z, x * NZ + (z + d) % NZ) for x in range(NX) for z in range(NZ)]
    return lax.ppermute(value, "section", pairs)


def shift_x(value, d):
    pairs = [(x * NZ + z, ((x + d) % NX) * NZ + z) for x in range(NX) for z in range(NZ)]
    return lax.ppermute(value, "section", pairs)


def in_order(relative, own, count):
    held = jnp.stack(relative)
    return jnp.concatenate(
        [lax.dynamic_index_in_dim(held, (own - j) % count, 0, keepdims=False) for j in range(count)],
        axis=1,
    )


def spread_x(value, extra, own):
    parts = value.reshape(value.shape[0], NX, -1).transpose(1, 0, 2)

    def part(d):
        return lax.dynamic_index_in_dim(parts, (own + d) % NX, 0, keepdims=False)

    sent = [
        shift_x(jnp.concatenate([part(d).astype(bf16), extra]), d).astype(f32) for d in range(1, NX)
    ]
    total = sum(sent, jnp.concatenate([part(0), extra.astype(f32)]))
    return total[: value.shape[0]], total[value.shape[0] :]


def high_low(value):
    high = value.astype(bf16)
    return high, (value - high.astype(f32)).astype(bf16)


def spread_z_far(value, own):
    parts = value.reshape(value.shape[0], NZ, -1).transpose(1, 0, 2)

    def part(d):
        return lax.dynamic_index_in_dim(parts, (own + d) % NZ, 0, keepdims=False)

    above = shift_z(jnp.stack([part(2), part(3), part(4)]).astype(bf16), 3)
    below = shift_z(jnp.stack([part(-3), part(-2)]).astype(bf16), -3)
    return part(-1), part(0), part(1), above, below


def spread_z_near(behind, here, ahead, above, below):
    above, below = above.astype(f32), below.astype(f32)
    right = shift_z((ahead + above[2] + below[1]).astype(bf16), 1)
    left = shift_z((behind + above[0]).astype(bf16), -1)
    return here + above[1] + below[0] + right.astype(f32) + left.astype(f32)


def ring_gather_x(value):
    half = value.shape[1] // 2
    a, b = value[:, :half], value[:, half:]
    below_a, above_b = shift_x(a, 1), shift_x(b, -1)
    below_b, above_a = shift_x(b, 1), shift_x(a, -1)
    far_a, far_b = shift_x(below_a, 1), shift_x(above_b, -1)
    return [(a, b), (below_a, below_b), (far_a, far_b), (above_a, above_b)]


def ring_scatter_x(parts, far):
    far_a, far_b = far
    below_b, above_a = shift_x(parts[1][1], 1), shift_x(parts[3][0], -1)
    next_a = (parts[1][0].astype(f32) + far_a.astype(f32)).astype(bf16)
    next_b = (parts[3][1].astype(f32) + far_b.astype(f32)).astype(bf16)
    below_a, above_b = shift_x(next_a, 1), shift_x(next_b, -1)
    return [(below_a, below_b), (above_a, above_b)]


def near_z(value):
    return jnp.stack([shift_z(value, 1), value, shift_z(value, -1)])


def far_z(near):
    low, high = shift_z(near, 3), shift_z(near[:2], -3)
    return [low, near, high]


def side_by_side(pieces, own):
    held = jnp.concatenate(pieces)
    return jnp.concatenate(
        [
            lax.dynamic_index_in_dim(held, (j - own + 4) % NZ, 0, keepdims=False)
            for j in range(NZ)
        ],
        axis=1,
    )


def dot_nt(a, b):
    return lax.dot_general(a, b, (((1,), (1,)), ((), ())), preferred_element_type=f32)


def dot_tn(a, b):
    return lax.dot_general(a, b, (((0,), (0,)), ((), ())), preferred_element_type=f32)


def weights_by_z(w_ref, gate_ref, up_ref):
    ff = gate_ref.shape[-1]
    for j in range(PAIR):
        block = slice(j * w_ref.shape[0] // PAIR, (j + 1) * w_ref.shape[0] // PAIR)
        w_ref[block, :ff] = gate_ref[:, j].reshape(-1, ff)
        w_ref[block, ff:] = up_ref[:, j].reshape(-1, ff)


def forward_kernel(
    x_ref, tok_ref, gate_ref, up_ref, coef_ref, silu_ref, hid_ref, acc, weights
):
    step = pl.program_id(0)
    ff = gate_ref.shape[-1]

    @pl.when(step == 0)
    def _():
        acc[...] = jnp.zeros_like(acc)

    weights_by_z(weights, gate_ref, up_ref)
    cut = tok_ref.shape[2]
    acc[...] += sum(
        jnp.dot(tok_ref[j], weights[j * cut : (j + 1) * cut], preferred_element_type=f32)
        for j in range(PAIR)
    )

    @pl.when(step == NZ // PAIR - 1)
    def _():
        act_gate, act_up = acc[:, :ff], acc[:, ff:]
        sig = jax.nn.sigmoid(act_gate)
        silu_gate = act_gate * sig
        silu_ref[...] = silu_gate
        coef_ref[...] = act_up * (sig * (1.0 + act_gate * (1.0 - sig)))
        hid_ref[...] = (silu_gate * act_up).astype(bf16)


def output_kernel(x_ref, hid_ref, down_ref, *rest):
    outs, made = rest[:-1], rest[-1]
    step = pl.program_id(0)
    made[...] = jnp.dot(hid_ref[...], down_ref[...], preferred_element_type=f32).astype(bf16)

    for d in range(len(outs) // 2):

        @pl.when(step == d)
        def _(d=d):
            half = made.shape[1] // 2
            outs[2 * d][...] = made[:, :half]
            outs[2 * d + 1][...] = made[:, half:]


def early_kernel(x_ref, *refs):
    ups, (down_ref, sum_ref, piece) = refs[: 2 * NX - 2], refs[2 * NX - 2 :]
    step = pl.program_id(0)

    for d in range(NX - 1):

        @pl.when(step == d)
        def _(d=d):
            half = piece.shape[1] // 2
            piece[:, :half] = ups[2 * d][...]
            piece[:, half:] = ups[2 * d + 1][...]

    @pl.when(step == 0)
    def _():
        sum_ref[...] = jnp.zeros_like(sum_ref)

    sum_ref[...] += dot_nt(piece[...], down_ref[...])


def backward_kernel(x_ref, *refs):
    far_a, far_b, down_ref, sum_ref, gate_ref, up_ref, coef_ref, silu_ref, hid_ref = refs[:9]
    part_ref, act_out, mix, weights = refs[9:]
    step = pl.program_id(0)
    width = gate_ref.shape[-1]
    rows = sum_ref.shape[0]

    @pl.when(step == 0)
    def _():
        half = down_ref.shape[1] // 2
        grad_hidden = sum_ref[...] + dot_nt(far_a[...], down_ref[:, :half])
        grad_hidden += dot_nt(far_b[...], down_ref[:, half:])
        act_out[:, :width] = (grad_hidden * coef_ref[...]).astype(bf16)
        act_out[:, width:] = (grad_hidden * silu_ref[...]).astype(bf16)
        terms = grad_hidden * hid_ref[...].astype(f32)
        sums = lax.dot_general(
            jnp.ones((8, width), f32),
            terms,
            (((1,), (1,)), ((), ())),
            precision=highest,
            preferred_element_type=f32,
        )
        high, low = high_low(sums)
        cut = part_ref.shape[2]
        tail = jnp.zeros((1, 2 * cut - rows), bf16)
        mix[...] = jnp.concatenate(
            [
                high[:1, :cut],
                jnp.concatenate([high[:1, cut:], tail], axis=1),
                low[:1, :cut],
                jnp.concatenate([low[:1, cut:], tail], axis=1),
                jnp.zeros((4, cut), bf16),
            ]
        )

    @pl.when(step >= 1)
    def _():
        weights_by_z(weights, gate_ref, up_ref)
        part = dot_nt(act_out[...], weights[...]).astype(bf16)
        cut = part_ref.shape[2]
        for j in range(PAIR):
            part_ref[j, :rows] = part[:, j * cut : (j + 1) * cut]
            part_ref[j, rows:] = mix[...]


def weight_kernel(x_ref, *refs):
    tok_ref, act_ref, hid_ref = refs[:3]
    ups = refs[3 : 3 + 2 * NX]
    gate_out, up_out, down_out, piece = refs[3 + 2 * NX :]
    step = pl.program_id(0)
    first = NZ // PAIR
    ff = hid_ref.shape[1]

    @pl.when(step < first)
    def _():
        for j in range(PAIR):
            block = dot_tn(tok_ref[j], act_ref[...]).astype(bf16)
            gate_out[:, j] = block[:, :ff].reshape(NX, -1, ff)
            up_out[:, j] = block[:, ff:].reshape(NX, -1, ff)

    for d in range(NX):

        @pl.when(step == first + d)
        def _(d=d):
            half = piece.shape[1] // 2
            piece[:, :half] = ups[2 * d][...]
            piece[:, half:] = ups[2 * d + 1][...]

    @pl.when(step >= first)
    def _():
        down_out[...] = dot_tn(hid_ref[...], piece[...]).astype(bf16)


def call(kernel, steps, in_specs, out_specs, out_shape, scratch, flops, moved, args):
    return pl.pallas_call(
        kernel,
        grid_spec=pltpu.PrefetchScalarGridSpec(
            num_scalar_prefetch=1,
            grid=(steps,),
            in_specs=in_specs,
            out_specs=out_specs,
            scratch_shapes=scratch,
        ),
        out_shape=out_shape,
        compiler_params=pltpu.CompilerParams(vmem_limit_bytes=63 * 1024 * 1024),
        cost_estimate=pl.CostEstimate(flops=flops, bytes_accessed=moved, transcendentals=0),
    )(*args)


def slot_tables(route_rows, mix_rows, capacity, experts):
    tok_count, top_count = route_rows.shape
    flat_routes = route_rows.reshape(-1)
    onehot = flat_routes[:, None] == jnp.arange(experts, dtype=jnp.int32)[None, :]
    count = tok_count * top_count
    pairs = jnp.arange(count, dtype=jnp.int32)
    before = (pairs[None, :] < pairs[:, None]).astype(bf16)
    earlier = jnp.dot(before, onehot.astype(bf16), preferred_element_type=f32)
    position = jnp.sum(jnp.where(onehot, earlier, 0.0), axis=1).astype(jnp.int32)
    target = (flat_routes * capacity + position).reshape(tok_count, top_count)
    slot_ids = jnp.arange(experts * capacity, dtype=jnp.int32)
    hits = target.T[None, :, :] == slot_ids[:, None, None]
    matches = hits.astype(f32)
    select = jnp.sum(matches, axis=1)
    weighted = jnp.sum(matches * mix_rows.T[None, :, :], axis=1)
    picks = matches.astype(bf16).reshape(experts * capacity, -1)
    return (select.astype(bf16), weighted, picks)


def per_device(tokens, routes, mix_weights, w_gate, w_up, w_down, upstream):
    experts = lax.axis_size("expert")
    section = lax.axis_index("section")
    my_x, my_z = section // NZ, section % NZ
    tok_count, feat = tokens.shape
    top_count = routes.shape[1]
    capacity = 5 * tok_count * top_count // (4 * experts)
    rows = experts * capacity
    ff = w_gate.shape[2]
    wide_x, wide_z = NX * feat, NZ * feat
    full = NX * wide_z
    where = my_x.reshape(1).astype(jnp.int32)
    gate4 = w_gate.reshape(NX, NZ, feat, ff)
    up4 = w_up.reshape(NX, NZ, feat, ff)
    down = w_down[0]

    up_near = near_z(upstream)
    select_low, weighted, picks = slot_tables(routes, mix_weights, capacity, experts)
    slot_scale = jnp.sum(weighted, axis=1)

    def exchange(value):
        return lax.all_to_all(
            value.reshape(experts, -1, value.shape[-1]), "expert", split_axis=0, concat_axis=0, tiled=True
        ).reshape(-1, value.shape[-1])

    tok_sent = jnp.dot(select_low, tokens, preferred_element_type=f32).astype(bf16)
    tok_sent, up_near = lax.optimization_barrier((tok_sent, up_near))
    up_pieces = far_z(up_near)
    tok_rows, up_pieces = lax.optimization_barrier((exchange(tok_sent), up_pieces))
    tok_x = in_order([tok_rows] + [shift_x(tok_rows, d) for d in range(1, NX)], my_x, NX)
    up_z = side_by_side(up_pieces, my_z)
    up_rows = jnp.dot(select_low, up_z, preferred_element_type=f32) * slot_scale[:, None]
    up_rows = exchange(up_rows.astype(bf16))

    dispatched = lax.all_gather(
        tok_x, "section", axis_index_groups=Z_GROUPS, axis=0, tiled=False
    )
    ups = [half for pair in ring_gather_x(up_rows) for half in pair]

    def whole(*shape):
        return pl.BlockSpec(shape, lambda i, s: (0,) * len(shape))

    def clip(i, low, count):
        return jnp.clip(i - low, 0, count - 1)

    def weight_spec(low):
        return pl.BlockSpec(
            (NX, PAIR, feat, ff), lambda i, s: (0, clip(i, low, NZ // PAIR), 0, 0)
        )

    def struct(shape, kind):
        return jax.ShapeDtypeStruct(shape, kind)

    tok_spec = pl.BlockSpec((PAIR, rows, wide_x), lambda i, s: (clip(i, 0, NZ // PAIR), 0, 0))
    weight_scratch = pltpu.VMEM((PAIR * wide_x, 2 * ff), bf16)
    (early,) = call(
        early_kernel,
        NX - 1,
        [whole(rows, wide_z // 2)] * (2 * NX - 2)
        + [
            pl.BlockSpec(
                (ff, wide_z), lambda i, s: (0, (s[0] + jnp.where(i == 1, NX - 1, i // 2)) % NX)
            )
        ],
        [whole(rows, ff)],
        [struct((rows, ff), f32)],
        [pltpu.VMEM((rows, wide_z), bf16)],
        0,
        0,
        (where, *ups[:4], *ups[6:], down),
    )
    dispatched, early = lax.optimization_barrier((dispatched, early))
    coef, silu_gate, hidden = call(
        forward_kernel,
        NZ // PAIR,
        [tok_spec, weight_spec(0), weight_spec(0)],
        [whole(rows, ff)] * 3,
        [struct((rows, ff), f32)] * 2 + [struct((rows, ff), bf16)],
        [pltpu.VMEM((rows, 2 * ff), f32), weight_scratch],
        4 * rows * full * ff,
        2 * (rows * full + 2 * full * ff),
        (where, dispatched, gate4, up4),
    )

    def outputs(hidden, steps, place):
        outs = call(
            output_kernel,
            steps,
            [
                whole(rows, ff),
                pl.BlockSpec((ff, wide_z), lambda i, s: (0, (s[0] + place(i)) % NX)),
            ],
            [whole(rows, wide_z // 2)] * (2 * steps),
            [struct((rows, wide_z // 2), bf16)] * (2 * steps),
            [pltpu.VMEM((rows, wide_z), bf16)],
            0,
            0,
            (where, hidden, down),
        )
        return [(outs[2 * d], outs[2 * d + 1]) for d in range(steps)]

    (farthest,) = outputs(hidden, 1, lambda i: 2)
    far = shift_x(farthest[0], 1), shift_x(farthest[1], -1)

    back, grad_act = call(
        backward_kernel,
        1 + NZ // PAIR,
        [whole(rows, wide_z // 2)] * 2
        + [pl.BlockSpec((ff, wide_z), lambda i, s: (0, (s[0] + 2) % NX))]
        + [whole(rows, ff)]
        + [weight_spec(1)] * 2
        + [whole(rows, ff)] * 3,
        [
            pl.BlockSpec(
                (PAIR, rows + 8, wide_x), lambda i, s: (clip(i, 1, NZ // PAIR), 0, 0)
            ),
            whole(rows, 2 * ff),
        ],
        [struct((NZ, rows + 8, wide_x), bf16), struct((rows, 2 * ff), bf16)],
        [pltpu.VMEM((8, wide_x), bf16), weight_scratch],
        0,
        0,
        (where, *ups[4:6], down, early, gate4, up4, coef, silu_gate, hidden),
    )

    hidden, grad_act = lax.optimization_barrier((hidden, grad_act))
    own, above, below = outputs(hidden, 3, lambda i: i + i // 2)
    back, far, own, above, below = lax.optimization_barrier((back, far, own, above, below))
    outs = [own, above, None, below]
    sent_x = ring_scatter_x(outs, far)

    back_z = lax.psum_scatter(
        back.reshape(NZ * (rows + 8), wide_x),
        "section",
        axis_index_groups=Z_GROUPS,
        scatter_dimension=0,
        tiled=True,
    )
    grad_gate, grad_up, grad_down = call(
        weight_kernel,
        NZ // PAIR + NX,
        [tok_spec, whole(rows, 2 * ff), whole(rows, ff)]
        + [whole(rows, wide_z // 2)] * (2 * NX),
        [weight_spec(0)] * 2
        + [pl.BlockSpec((ff, wide_z), lambda i, s: (0, (s[0] + NX - clip(i, NZ // PAIR, NX)) % NX))],
        [struct((NX, NZ, feat, ff), bf16)] * 2 + [struct((ff, full), bf16)],
        [pltpu.VMEM((rows, wide_z), bf16)],
        0,
        0,
        (where, dispatched, grad_act, hidden, *ups),
    )

    sent_x, grads = lax.optimization_barrier((sent_x, (grad_gate, grad_up, grad_down)))
    grad_gate, grad_up, grad_down = grads

    summed = jnp.concatenate(
        [
            (outs[0][h].astype(f32) + sent_x[0][h].astype(f32) + sent_x[1][h].astype(f32)).astype(bf16)
            for h in range(2)
        ],
        axis=1,
    )
    returned = exchange(summed)
    moe_out = jnp.dot(weighted.T, returned.astype(f32), precision=highest)
    moe_out, back_z = lax.optimization_barrier((moe_out, back_z))

    mix = back_z[rows : rows + 4].reshape(2, 2 * wide_x)[:, :rows].reshape(2, experts, capacity)
    mix = jnp.pad(mix.transpose(1, 0, 2), ((0, 0), (0, 6), (0, wide_x - capacity)))
    back = exchange(
        jnp.concatenate([back_z[:rows].reshape(experts, capacity, wide_x), mix], axis=1)
    ).reshape(experts, capacity + 8, wide_x)
    moe_parts, back = lax.optimization_barrier((spread_z_far(moe_out, my_z), back))
    mixed = (tokens.astype(f32) + spread_z_near(*moe_parts)).astype(bf16)
    grad_moe = dot_tn(select_low, back[:, :capacity].reshape(rows, wide_x))
    mix = back[:, capacity : capacity + 2, :capacity].transpose(1, 0, 2).reshape(2, rows)
    mix = jnp.sum(jnp.dot(mix, picks, preferred_element_type=f32), axis=0).reshape(-1, feat)
    grad_moe, mix = spread_x(grad_moe, jnp.concatenate(high_low(mix)), my_x)
    grad_tokens = (upstream.astype(f32) + grad_moe).astype(bf16)
    mix = jnp.sum(mix.reshape(2, top_count, tok_count), axis=0)
    grad_mix = mix.T / mix_weights
    return (
        mixed,
        grad_tokens,
        grad_mix,
        grad_gate.reshape(1, full, ff),
        grad_up.reshape(1, full, ff),
        grad_down[None],
    )


def solution(mesh):
    return jax.shard_map(
        per_device,
        mesh=mesh,
        in_specs=(
            P("expert", "section"),
            P("expert", None),
            P("expert", None),
            P("expert", None, "section"),
            P("expert", None, "section"),
            P("expert", "section", None),
            P("expert", "section"),
        ),
        out_specs=(
            P("expert", "section"),
            P("expert", "section"),
            P("expert", None),
            P("expert", None, "section"),
            P("expert", None, "section"),
            P("expert", "section", None),
        ),
        check_vma=False,
    )
```
